128 devices in a mesh: lat: 8 (over x_hi, y), grp: 16 (over z, x_lo, core).
Axes of the slice: x: 4 (x_hi: 2, x_lo: 2; x = x_hi * 2 + x_lo), y: 4, z: 4, core: 2. Of those that a mesh axis runs over, the one named last changes fastest.
Arguments:
- fields: float32 [512, 30, 64, 128], P('grp', None, 'lat'), may hold values from -6 to 6
- diffusion: float32 [64, 128], P('lat'), may hold values from 0.12 to 0.245
- mixing: float32 [30, 30], replicated, may hold values from -0.08 to 1
- heating: float32 [30, 64, 128], P(None, 'lat'), may hold values from -2 to 2
- land_mask: int32 [64, 128], P('lat'), may hold values 0 or 1
- conv_weight: float32 [32, 27], replicated, may hold values from -1.25 to 1.25
- head_weight: float32 [32, 64, 128], P(None, 'lat'), may hold values from -0.01171875 to 0.01171875
- counts: int32 [512], replicated, may hold values from 0 to 32, as said below
- source: int32 [512], replicated, may hold values from 0 to 511, as said below
Outputs:
- new_fields: float32 [512, 30, 64, 128], P('grp', None, 'lat')
- scores: float32 [512], P('grp')
- slot_weight: float32 [512], P('grp')
The draws below stay inside these ranges and needn't reach their ends.
Inputs may be any that keep to these rules, and one draw needn't show every extreme that they name: Members 32 g to 32 g + 31 form group g. In every group exactly one member has a count of 2 or more and every group has a member of count 0; the counts sum to 512. source[s] = s where the member s has a count of 1 or more. Every slot s of count 0 takes the member of count 2 or more of one other group, the same group for all such slots of s's group, each group's such member is taken by the slots of exactly one other group, and a member of count c is taken by c - 1 slots.
All inputs are finite; a program needn't handle non-finite values. No bound on the sum of `land_mask` on one device may be relied on, other than what follows from the above.
Results may differ from the reference program's by a relative error of at most 0.0003.
Values sent between devices are 32-bit elements; how exact they have to be, the bound alone decides.
No kernel may reach another device: no remote copies, remote signals or barrier semaphores. Data moves between devices by JAX's collectives and lax.ppermute only.
A program may use at most 128 MiB of HBM per device.

```python
import math
import jax
import jax.numpy as jnp
from jax import lax

NLON = 128
NLAT = 64
LEV = 10
FLD = 3
CH = 32
MEM_GRP = 32
STEPS = 4
MEMBERS = 512


def clone_plan(key):
    base_key = jax.random.fold_in(key, 911)
    key_hot, key_extra, key_order, key_force, key_rotate = jax.random.split(base_key, 5)
    groups = MEMBERS // MEM_GRP
    hot_slot = jax.random.randint(key_hot, (groups,), 0, MEM_GRP)
    extra = jax.random.randint(key_extra, (groups,), 1, MEM_GRP)
    forced = jax.random.randint(key_force, (), 0, groups)
    extra = jnp.where(jnp.arange(groups) == forced, MEM_GRP - 1, extra)
    order = jax.random.permutation(key_order, groups)
    before = jnp.zeros((groups,), jnp.int32).at[order].set(jnp.roll(order, 1).astype(jnp.int32))
    killed_count = extra[before]
    rotate = jax.random.randint(key_rotate, (groups,), 0, MEM_GRP - 1)
    slots = jnp.arange(MEM_GRP)
    relative = (slots[None, :] - hot_slot[:, None]) % MEM_GRP
    ranking = (relative - 1 - rotate[:, None]) % (MEM_GRP - 1)
    is_killed = (relative > 0) & (ranking < killed_count[:, None])
    is_hot = relative == 0
    counts = jnp.where(is_hot, 1 + extra[:, None], jnp.where(is_killed, 0, 1)).reshape(-1)
    donor = before * MEM_GRP + hot_slot[before]
    own_slot = jnp.arange(MEMBERS).reshape(groups, MEM_GRP)
    source = jnp.where(is_killed, donor[:, None], own_slot).reshape(-1)
    return (counts.astype(jnp.int32), source.astype(jnp.int32))


def draw_counts(key, part):
    return clone_plan(key)[0]


def draw_source(key, part):
    return clone_plan(key)[1]


def draw_mixing(key, part):
    key_diag, key_off = jax.random.split(jax.random.fold_in(key, 313))
    order_size = FLD * LEV
    diagonal = jax.random.uniform(key_diag, (order_size,), jnp.float32, 0.85, 1.0)
    offside = jax.random.uniform(key_off, (order_size, order_size), jnp.float32, -0.08, 0.08)
    identity = jnp.eye(order_size, dtype=jnp.float32)
    return offside * (1.0 - identity) + identity * diagonal[None, :]


def touch_ends(array, key, smallest, largest):
    longest = array.shape.index(max(array.shape))
    spots = []
    for shift in (0, 1):
        where = [jax.random.randint(jax.random.fold_in(key, axis), (), 0, length) for axis, length in enumerate(array.shape)]
        where[longest] = (where[longest] + shift) % array.shape[longest]
        spots.append(tuple(where))
    return array.at[spots[0]].set(smallest).at[spots[1]].set(largest)


def shard_levels(key, extent, shards, low, top_value):
    loudness, own = 1.0, jax.random.fold_in(key, 6)
    for axis_at, shards_of in shards:
        heights = jnp.exp(jax.random.uniform(jax.random.fold_in(own, axis_at), (shards_of,), jnp.float32, low / len(shards), top_value / len(shards)))
        loudness = loudness * jnp.repeat(heights, extent[axis_at] // shards_of).reshape([-1 if axis == axis_at else 1 for axis in range(len(extent))])
    return loudness


def bell_draw(own_key, dims, deviation, reach, cuts=(), kind=jnp.bfloat16):
    drawn = jax.random.normal(own_key, dims, jnp.float32) * deviation
    if len(cuts) > 0:
        drawn = shard_levels(own_key, dims, cuts, -0.22, 0.18) * drawn
    return jnp.clip(drawn, min=-reach, max=reach).astype(kind)


def setup_inputs(seed: int = 0) -> dict:
    key_of = jax.random.split(jax.random.key(seed), 10)
    fields = bell_draw(key_of[0], (MEMBERS, FLD * LEV, NLAT, NLON), 1.0, 6.0, ((0, 16), (2, 8)), jnp.float32)
    diffusion = jnp.clip(jnp.exp(math.log(0.245) - 0.7137665 * jax.random.uniform(key_of[1], (NLAT, NLON), jnp.float32) ** shard_levels(key_of[1], (NLAT, NLON), ((0, 8),), -0.2, 0.2)), 0.12, 0.245)
    mixing = draw_mixing(jax.random.fold_in(key_of[9], 71), 0)
    heating = bell_draw(key_of[3], (FLD * LEV, NLAT, NLON), 0.3, 2.0, ((1, 8),), jnp.float32)
    land_mask = touch_ends((jax.random.randint(key_of[4], (NLAT, NLON), 0, 3) < 1).astype(jnp.int32), jax.random.fold_in(key_of[4], 1), 0, 1)
    conv_weight = bell_draw(key_of[5], (CH, 27), 27 ** -0.5, 1.25, (), jnp.float32)
    head_weight = bell_draw(key_of[6], (CH, NLAT, NLON), (CH * NLAT * NLON) ** -0.5, 0.01171875, ((1, 8),), jnp.float32)
    counts = draw_counts(jax.random.fold_in(key_of[9], 71), 0)
    source = draw_source(jax.random.fold_in(key_of[9], 71), 0)
    return dict(fields=fields, diffusion=diffusion, mixing=mixing, heating=heating, land_mask=land_mask, conv_weight=conv_weight, head_weight=head_weight, counts=counts, source=source)


def advance(values, diffusion, mixing, heating):
    padded = jnp.pad(values, ((0, 0), (0, 0), (1, 1), (0, 0)))
    laplace = padded[:, :, 2:] + padded[:, :, :-2] + jnp.roll(values, 1, 3) + jnp.roll(values, -1, 3) - 4.0 * values
    smooth = values + diffusion * laplace
    mixed = jnp.einsum('ij,mjac->miac', mixing, smooth, precision=lax.Precision.HIGHEST)
    return mixed + heating - 0.05 * mixed * mixed * mixed


def surface_inputs(final, land_mask):
    land_float = land_mask.astype(jnp.float32)
    temper = final[:, 0]
    moisture = final[:, LEV]
    return jnp.stack([temper * land_float, moisture, temper * (1.0 - land_float)], 1)


def score_terms(padded, conv_weight, head_weight):
    height = padded.shape[2] - 2
    members_here = padded.shape[0]
    taps = [jnp.roll(padded[:, :, shift_lat:shift_lat + height], -shift_lon, 3) for shift_lat in range(3) for shift_lon in (-1, 0, 1)]
    patches = jnp.stack(taps, 2).reshape(members_here, 27, height * padded.shape[3])
    hidden = jax.nn.relu(jnp.einsum('ck,mkp->mcp', conv_weight, patches, precision=lax.Precision.HIGHEST))
    return jnp.einsum('mcp,cp->m', hidden, head_weight.reshape(head_weight.shape[0], -1), precision=lax.Precision.HIGHEST)


def reference(fields, diffusion, mixing, heating, land_mask, conv_weight, head_weight, counts, source):
    final = fields
    for repeat in range(STEPS):
        final = advance(final, diffusion, mixing, heating)
    inputs = surface_inputs(final, land_mask)
    padded = jnp.pad(inputs, ((0, 0), (0, 0), (1, 1), (0, 0)))
    scores = score_terms(padded, conv_weight, head_weight)
    weights = jnp.exp(scores)
    weights = weights / jnp.mean(weights)
    new_fields = final[source]
    slot_weight = weights[source] / counts[source].astype(jnp.float32)
    return new_fields, scores, slot_weight
```

```python
import functools

import jax
import jax.numpy as jnp
import numpy as np
from jax import lax
from jax.experimental import pallas as pl
from jax.experimental.pallas import tpu as pltpu
from jax.sharding import PartitionSpec as P


LEV = 10
STEPS = 4
STARTS = (0, 8, 16, 22)
DEEP_A = 4
DEEP_B = 5
NA = 20
NB = 32 - NA
BLK = 4
PARAMS = 160
MID = 2 * NA + 120
SCALE = 0.05**0.5
LAG = 4


VMEM = pltpu.VMEM
ANY = pl.ANY
WHOLE = pl.BlockSpec(memory_space=pltpu.VMEM)
SCALAR = pl.BlockSpec(memory_space=pltpu.SMEM)


def split(value):
    high = value.astype(jnp.bfloat16)
    low = (value - high.astype(jnp.float32)).astype(jnp.bfloat16)
    return high, low


def strided_row(ref, base, row, stride):
    parts = [ref[pl.ds(base + start * stride + row, 8, stride=stride), :] for start in STARTS]
    return jnp.concatenate(parts, 0)


def strided_store(ref, row, value):
    for k, start in enumerate(STARTS):
        ref[pl.ds(start * 8 + row, 8, stride=8), :] = value[8 * k : 8 * k + 8]


def first_rows(depth, up_ref, base_up, own_ref, down_ref, base_down):
    def first_row(row):
        if row < depth:
            return strided_row(up_ref, base_up, row, depth)
        if row < depth + 8:
            return strided_row(own_ref, 0, row - depth, 8)
        return strided_row(down_ref, base_down, row - depth - 8, depth)

    return first_row


def emit_pair(member, step, pair, coef, heat, lefts, depth):
    first_row, state, store_last = member
    row = step + 2 * pair
    last = step == STEPS
    shift = DEEP_B - depth

    def load(at):
        if step == 1:
            return first_row(at)
        return state[step % 2][pl.ds(at * 32, 32), :]

    rows = [load(at) for at in range(row - 1, row + 3)]
    smooth = []
    for i in (0, 1):
        here = rows[i + 1]
        at = row + i + shift
        total = (rows[i] + rows[i + 2]) + (pltpu.roll(here, 1, 1) + pltpu.roll(here, 127, 1))
        keep = coef[0, pl.ds(at * 8, 8), :]
        diff = coef[1, pl.ds(at * 8, 8), :]
        smooth.append(jnp.concatenate([keep] * 4, 0) * here + jnp.concatenate([diff] * 4, 0) * total)
    high, low = split(jnp.concatenate(smooth, 1))
    right = jnp.concatenate([high, high, low], 0)
    mixed = jnp.dot(lefts[0 if step == 1 else 2 if last else 1], right, preferred_element_type=jnp.float32)
    for i in (0, 1):
        at = row + i
        part = mixed[:, 128 * i : 128 * (i + 1)]
        warm = heat[1 if last else 0, pl.ds((at + shift) * 32, 32), :]
        if last:
            store_last(at - depth, part * (1.0 - 0.05 * (part * part)) + warm)
        else:
            state[(step + 1) % 2][pl.ds(at * 32, 32), :] = part * (1.0 - part * part) + warm


def run_members(members, coef, heat, lefts, depth):
    count = {step: depth + 4 - step for step in range(1, STEPS + 1)}
    for wave in range(count[1] + LAG * (STEPS - 1) + 1):
        for step in range(1, STEPS + 1):
            pair = wave - LAG * (step - 1)
            if 0 <= pair < count[step]:
                for member in members:
                    emit_pair(member, step, pair, coef, heat, lefts, depth)


def prepare(pup_ref, pdown_ref, hown_ref, diff_ref, mix_ref, coef, heat, lefts):
    for row in range(18):
        if row < 5:
            value = strided_row(pup_ref, 0, row, 5)
            diff = pup_ref[pl.ds(150 + row, 1), :]
        elif row < 13:
            value = strided_row(hown_ref, 0, row - 5, 8)
            diff = diff_ref[pl.ds(row - 5, 1), :]
        else:
            value = strided_row(pdown_ref, 0, row - 13, 5)
            diff = pdown_ref[pl.ds(150 + row - 13, 1), :]
        heat[1, pl.ds(row * 32, 32), :] = value
        heat[0, pl.ds(row * 32, 32), :] = SCALE * value
        diff = jnp.broadcast_to(diff, (8, 128))
        coef[1, pl.ds(row * 8, 8), :] = diff
        coef[0, pl.ds(row * 8, 8), :] = 1.0 - 4.0 * diff
    mix = mix_ref[...]
    for i, factor in enumerate((SCALE, 1.0, 1.0 / SCALE)):
        high, low = split(factor * mix)
        lefts[i] = jnp.concatenate([high, low, high], 1)


def keep_scored(tq_ref, j, out):
    tq_ref[j, 0:8, :] = out[0:8, :]
    tq_ref[j, 8:16, :] = out[8 * LEV : 8 * LEV + 8, :]


def chunk_a_kernel(
    f_ref, up_ref, down_ref, pup_ref, pdown_ref, hown_ref, diff_ref, mix_ref, out_ref, tq_ref, coef, heat, lefts, *states
):
    @pl.when(pl.program_id(0) == 0)
    def _():
        prepare(pup_ref, pdown_ref, hown_ref, diff_ref, mix_ref, coef, heat, lefts)

    def one(p, carry):
        members = []
        for q in range(2):
            j = p * 2 + q
            base = pl.multiple_of(j * 120, 8)
            rows = first_rows(DEEP_A, up_ref, base, f_ref.at[j], down_ref, base)
            members.append((rows, states[2 * q : 2 * q + 2], functools.partial(strided_store, out_ref.at[j])))
        run_members(members, coef, heat, lefts, DEEP_A)
        for q in range(2):
            keep_scored(tq_ref, p * 2 + q, out_ref.at[p * 2 + q])
        return carry

    lax.fori_loop(0, BLK // 2, one, 0)


def chunk_b_kernel(
    killed_ref, f_ref, up_ref, down_ref, dup_ref, ddown_ref, donor_ref, pup_ref, pdown_ref, hown_ref, diff_ref, mix_ref, prev_ref,
    out_ref, tq_ref, edge_ref, coef, heat, lefts, s0, s1, s2, s3, final, donor, sems,
):
    i = pl.program_id(0)
    states = (s0, s1, s2, s3)

    def copy(m, source):
        return pltpu.make_async_copy(source, out_ref.at[m], sems.at[m])

    @pl.when(i == 0)
    def _():
        prepare(pup_ref, pdown_ref, hown_ref, diff_ref, mix_ref, coef, heat, lefts)
        rows = first_rows(DEEP_A, dup_ref, 2 * NA, donor_ref, ddown_ref, 2 * NA)
        run_members([(rows, states[:2], functools.partial(strided_store, donor))], coef, heat, lefts, DEEP_A)
        for m in range(NA):
            @pl.when(killed_ref[m] > 0)
            def _():
                copy(m, donor).start()

    def store_last(j, out, row, value):
        if 0 <= row < 8:
            strided_store(out, row, value)
            return
        slot = 0 if row < 0 else 3
        t, q = value[0:1], value[LEV : LEV + 1]
        edge_ref[j, slot : slot + 1, :] = t
        edge_ref[j, slot + 1 : slot + 2, :] = q
        edge_ref[j, slot + 2 : slot + 3, :] = t

    def one(p, carry):
        members = []
        for q in range(2):
            j = p * 2 + q
            base = j * (30 * DEEP_B)
            out = final.at[i * BLK + j]
            rows = first_rows(DEEP_B, up_ref, base, f_ref.at[j], down_ref, base)
            edge_ref[j] = jnp.zeros((8, 128), jnp.float32)
            members.append((rows, states[2 * q : 2 * q + 2], functools.partial(store_last, j, out)))
        run_members(members, coef, heat, lefts, DEEP_B)
        for q in range(2):
            j = p * 2 + q
            at = i * BLK + j
            m = NA + at
            keep_scored(tq_ref, j, final.at[at])

            @pl.when(killed_ref[m] > 0)
            def _():
                copy(m, donor).start()

            @pl.when(killed_ref[m] <= 0)
            def _():
                copy(m, final.at[at]).start()

        return carry

    lax.fori_loop(0, BLK // 2, one, 0)

    @pl.when(i == pl.num_programs(0) - 1)
    def _():
        for m in range(32):
            if m < NA:
                @pl.when(killed_ref[m] > 0)
                def _():
                    copy(m, donor).wait()
            else:
                copy(m, donor).wait()


def send_rows(x_ref, up_ref, down_ref, base, depth):
    for row in range(depth):
        for start in STARTS:
            to = pl.ds(base + start * depth + row, 8, stride=depth)
            down_ref[to, :] = x_ref[pl.ds(start * 8 + row, 8, stride=8), :]
            up_ref[to, :] = x_ref[pl.ds(start * 8 + 8 - depth + row, 8, stride=8), :]


def send_members(f_ref, first, count, depth, up_ref, down_ref, buf, sems, before):
    fetches = [
        pltpu.make_async_copy(f_ref.at[pl.ds(first + k * BLK, BLK)], buf.at[pl.ds(k * BLK, BLK)], sems.at[k])
        for k in range(count // BLK)
    ]
    for fetch in fetches:
        fetch.start()
    before()

    for k, fetch in enumerate(fetches):
        fetch.wait()

        def one(j, carry):
            m = k * BLK + j
            send_rows(buf.at[m], up_ref, down_ref, m * (30 * depth), depth)
            return carry

        lax.fori_loop(0, BLK, one, 0)


def edges_a_kernel(me_ref, counts_ref, f_ref, heat_ref, diff_ref, land_ref, pieces_ref, up_ref, down_ref, buf, sems, hot_sem):
    me = me_ref[0]
    hot = lax.fori_loop(0, 32, lambda j, at: jnp.where(counts_ref[me * 32 + j] >= 2, j, at), 0)
    fetch = pltpu.make_async_copy(f_ref.at[hot], pieces_ref.at[pl.ds(0, 240)], hot_sem)
    fetch.start()

    def before():
        pieces_ref[240:256, :] = jnp.zeros((16, 128), jnp.float32)
        base = NA * 120
        send_rows(heat_ref, up_ref, down_ref, base, 5)
        diff = diff_ref[...]
        land = land_ref[...].astype(jnp.float32)
        up_ref[base + 150 : base + 155, :] = diff[3:]
        up_ref[base + 155 : base + 160, :] = land[3:]
        down_ref[base + 150 : base + 155, :] = diff[:5]
        down_ref[base + 155 : base + 160, :] = land[:5]

    send_members(f_ref, 0, NA, DEEP_A, up_ref, down_ref, buf, sems, before)
    fetch.wait()


def edges_b_kernel(f_ref, up_ref, down_ref, buf, sems):
    send_members(f_ref, NA, NB, DEEP_B, up_ref, down_ref, buf, sems, lambda: None)


def mid_kernel(donor_ref, tq_ref, up_ref, down_ref):
    for k in range(2 * NA // 8):
        up_ref[pl.ds(8 * k, 8), :] = tq_ref[pl.ds(64 * k + 7, 8, stride=8), :]
        down_ref[pl.ds(8 * k, 8), :] = tq_ref[pl.ds(64 * k, 8, stride=8), :]
    send_rows(donor_ref, up_ref, down_ref, 2 * NA, DEEP_A)


def pick_kernel(index_ref, pieces_ref, out_ref):
    for g in range(16):
        out_ref[g] = pieces_ref[index_ref[g]]


def edge_mask(pup_ref, pdown_ref):
    before, after = pup_ref[159:160, :], pdown_ref[155:156, :]
    one = jnp.ones((1, 128), jnp.float32)
    return jnp.concatenate([before, one, 1.0 - before, after, one, 1.0 - after, one, one], 0)


def score_members(count, tq_ref, edge_ref, land_ref, mask, weight_ref, head_ref, acc, first):
    land = land_ref[...].astype(jnp.float32)
    sea = 1.0 - land
    high, low = split(weight_ref[...])
    left = jnp.concatenate([high, low, high], 1)

    def pair(p, carry):
        cols = []
        for q in range(2):
            m = p * 2 + q
            t = tq_ref[m, 0:8, :]
            edge = edge_ref[pl.ds(pl.multiple_of(m * 8, 8), 8), :]
            value = jnp.concatenate([t * land, tq_ref[m, 8:16, :], t * sea, edge * mask], 0)
            cols.append(jnp.concatenate([pltpu.roll(value, 1, 1), value, pltpu.roll(value, 127, 1)], 0))
        h, l = split(jnp.concatenate(cols, 1))
        right = jnp.concatenate([h, h, l], 0)
        hidden = jnp.maximum(jnp.dot(left, right, preferred_element_type=jnp.float32), 0.0)
        head = head_ref[...]
        for q in range(2):
            part = (hidden[:, 128 * q : 128 * (q + 1)] * head).reshape(32, 8, 128)
            acc[pl.ds(first + p * 2 + q, 1), :] = jnp.sum(jnp.sum(part, 0), 0, keepdims=True)
        return carry

    lax.fori_loop(0, count // 2, pair, 0)


def score_a_kernel(tq_ref, before_ref, after_ref, pup_ref, pdown_ref, land_ref, weight_ref, head_ref, out_ref, edge):
    zero = jnp.zeros((8, 128), jnp.float32)
    for k in range((NA + 7) // 8):
        rows = [ref[pl.ds(16 * k + i, 8, stride=2), :] for ref in (before_ref, after_ref) for i in (0, 1)]
        for slot, value in enumerate((rows[0], rows[1], rows[0], rows[2], rows[3], rows[2], zero, zero)):
            edge[pl.ds(64 * k + slot, 8, stride=8), :] = value
    score_members(NA, tq_ref, edge, land_ref, edge_mask(pup_ref, pdown_ref), weight_ref, head_ref, out_ref, 0)


def score_b_kernel(tq_ref, edge_ref, pup_ref, pdown_ref, land_ref, weight_ref, head_ref, sums_ref, out_ref, acc):
    acc[0:NA, :] = sums_ref[...]
    score_members(NB, tq_ref, edge_ref, land_ref, edge_mask(pup_ref, pdown_ref), weight_ref, head_ref, acc, NA)
    ones = jnp.ones((8, 128), jnp.float32)
    padded = jnp.concatenate([acc[...], jnp.zeros((96, 128), jnp.float32)], 0)
    out_ref[...] = lax.dot_general(
        ones, padded, (((1,), (1,)), ((), ())), precision=lax.Precision.HIGHEST, preferred_element_type=jnp.float32
    )


def weight_kernel(me_ref, parts_ref, counts_ref, source_ref, scores_ref, slot_ref):
    me = me_ref[0]
    scores = jnp.sum(parts_ref[...].reshape(8, 16, 128), 0)[:, :32]
    weights = jnp.exp(scores)
    total = jnp.sum(weights)
    weights = weights / (total / 512.0)
    counts = counts_ref[...].astype(jnp.float32)
    group = lax.broadcasted_iota(jnp.int32, (16, 32), 0)
    member = lax.broadcasted_iota(jnp.int32, (16, 32), 1)
    flat = group * 32 + member
    source = source_ref[...]
    mine = group == me
    killed = jnp.logical_and(mine, source != flat)
    donor = jnp.max(jnp.where(killed, source, -1))
    here = flat == donor
    donor_weight = jnp.sum(jnp.where(here, weights, 0.0))
    donor_count = jnp.sum(jnp.where(here, counts, 0.0))
    top = jnp.where(killed, donor_weight, weights)
    under = jnp.where(killed, donor_count, counts)
    share = jnp.where(mine, top / jnp.where(mine, under, 1.0), 0.0)
    own = jnp.where(mine, scores, 0.0)
    scores_ref[...] = jnp.sum(own, 0, keepdims=True)
    slot_ref[...] = jnp.sum(share, 0, keepdims=True)


def spread_matrix():
    table = np.zeros((27, 8, 96), np.float32)
    for k in range(3):
        for a in (-1, 0, 1):
            for b in (-1, 0, 1):
                tap = 9 * k + 3 * (a + 1) + (b + 1)
                for i in range(8):
                    row = i + a
                    if 0 <= row < 8:
                        slot = 8 * k + row
                    elif row < 0:
                        slot = 24 + k
                    else:
                        slot = 27 + k
                    table[tap, i, (b + 1) * 32 + slot] = 1.0
    return table.reshape(27, 8 * 96)


def call(kernel, outs, **kw):
    return pl.pallas_call(kernel, out_shape=outs, **kw)


def f32(*shape):
    return jax.ShapeDtypeStruct(shape, jnp.float32)


def local(fields, diffusion, mixing, heating, land_mask, conv_weight, head_weight, counts, source):
    size = lax.axis_size("lat")
    up = [(i, i + 1) for i in range(size - 1)]
    down = [(i + 1, i) for i in range(size - 1)]
    me = lax.axis_index("grp").reshape(1).astype(jnp.int32)
    counts2 = counts.reshape(16, 32)
    source2 = source.reshape(16, 32)
    f = fields.reshape(32, 240, 128)
    heat = heating.reshape(240, 128)
    hbm = pl.BlockSpec(memory_space=ANY)

    def edge_scratch(count):
        return [VMEM((count, 240, 128), jnp.float32), pltpu.SemaphoreType.DMA((count // BLK,))]

    rows_a = NA * 120 + PARAMS
    pieces, send_up_a, send_down_a = call(
        edges_a_kernel,
        (f32(256, 128), f32(rows_a, 128), f32(rows_a, 128)),
        in_specs=[SCALAR, SCALAR, hbm, WHOLE, WHOLE, WHOLE],
        out_specs=(WHOLE,) * 3,
        scratch_shapes=edge_scratch(NA) + [pltpu.SemaphoreType.DMA],
        name="edges_a",
    )(me, counts, f, heat, diffusion, land_mask)

    pieces = lax.all_to_all(pieces.reshape(16, 16, 128), "grp", 0, 0, tiled=True)
    up_a = lax.ppermute(send_up_a, "lat", up)
    down_a = lax.ppermute(send_down_a, "lat", down)
    flat = jnp.arange(512, dtype=jnp.int32).reshape(16, 32)
    donor_group = jnp.max(jnp.where(source2 != flat, source2 // 32, 0), 1)
    pieces = call(pick_kernel, f32(16, 16, 128), in_specs=[SCALAR, WHOLE], out_specs=WHOLE, name="pick")(donor_group, pieces)
    donor_state = lax.all_to_all(pieces, "grp", 0, 0, tiled=True).reshape(256, 128)

    send_up_b, send_down_b = call(
        edges_b_kernel,
        (f32(NB * 150, 128), f32(NB * 150, 128)),
        in_specs=[hbm],
        out_specs=(WHOLE, WHOLE),
        scratch_shapes=edge_scratch(NB),
        name="edges_b",
    )(f)
    up_b = lax.ppermute(send_up_b, "lat", up)
    down_b = lax.ppermute(send_down_b, "lat", down)

    mix = jnp.concatenate([mixing[:24], mixing[22:]], 0)
    mix = jnp.concatenate([mix[:, :24], jnp.zeros((32, 2), jnp.float32), mix[:, 24:]], 1)
    taps = jnp.dot(conv_weight, jnp.asarray(spread_matrix()), precision=lax.Precision.HIGHEST).reshape(256, 96)
    head = head_weight.reshape(256, 128)
    killed = (lax.dynamic_index_in_dim(counts2, me[0], 0, keepdims=False) == 0).astype(jnp.int32)

    def whole(shape, at=0):
        return pl.BlockSpec(shape, lambda *i: (at,) + (0,) * (len(shape) - 1))

    params = whole((PARAMS, 128), NA * 120 // PARAMS)
    block = pl.BlockSpec((BLK, 240, 128), lambda i: (i, 0, 0))
    tq_block = pl.BlockSpec((BLK, 16, 128), lambda i: (i, 0, 0))
    step_scratch = [
        VMEM((2, 18 * 8, 128), jnp.float32),
        VMEM((2, 18 * 32, 128), jnp.float32),
        VMEM((3, 32, 96), jnp.bfloat16),
    ] + [VMEM((18 * 32, 128), jnp.float32)] * 4
    shared = [params, params, WHOLE, WHOLE, WHOLE]
    halo_a = pl.BlockSpec((BLK * 30 * DEEP_A, 128), lambda i: (i, 0))
    state_a, tq_a = call(
        chunk_a_kernel,
        (f32(32, 240, 128), f32(NA, 16, 128)),
        grid=(NA // BLK,),
        in_specs=[block, halo_a, halo_a] + shared,
        out_specs=(block, tq_block),
        scratch_shapes=step_scratch,
        name="chunk_a",
    )(f, up_a, down_a, up_a, down_a, heat, diffusion, mix)

    send_up, send_down = call(
        mid_kernel, (f32(MID, 128), f32(MID, 128)), in_specs=[WHOLE, WHOLE], out_specs=(WHOLE, WHOLE), name="mid"
    )(donor_state, tq_a.reshape(NA * 16, 128))
    before = lax.ppermute(send_up, "lat", up)
    after = lax.ppermute(send_down, "lat", down)

    sums_a = call(
        score_a_kernel,
        f32(NA, 128),
        grid=(1,),
        in_specs=[WHOLE] * 3 + [params] * 2 + [WHOLE] * 3,
        out_specs=WHOLE,
        scratch_shapes=[VMEM(((NA + 7) // 8 * 64, 128), jnp.float32)],
        name="score_a",
    )(tq_a, before, after, up_a, down_a, land_mask, taps, head)

    halo_b = pl.BlockSpec((BLK * 30 * DEEP_B, 128), lambda i: (i, 0))
    new_fields, tq_b, edge_b = call(
        chunk_b_kernel,
        (f32(32, 240, 128), f32(NB, 16, 128), f32(NB, 8, 128)),
        grid=(NB // BLK,),
        in_specs=[SCALAR, pl.BlockSpec((BLK, 240, 128), lambda i: (i + NA // BLK, 0, 0)), halo_b, halo_b]
        + [WHOLE] * 3
        + shared
        + [hbm],
        out_specs=(hbm, tq_block, pl.BlockSpec((BLK, 8, 128), lambda i: (i, 0, 0))),
        scratch_shapes=step_scratch
        + [VMEM((NB, 240, 128), jnp.float32), VMEM((240, 128), jnp.float32), pltpu.SemaphoreType.DMA((32,))],
        input_output_aliases={12: 0},
        name="chunk_b",
    )(killed, f, up_b, down_b, before, after, donor_state, up_a, down_a, heat, diffusion, mix, state_a)

    partial = call(
        score_b_kernel,
        f32(8, 128),
        grid=(1,),
        in_specs=[WHOLE] * 2 + [params] * 2 + [WHOLE] * 4,
        out_specs=WHOLE,
        scratch_shapes=[VMEM((32, 128), jnp.float32)],
        name="score_b",
    )(tq_b, edge_b.reshape(NB * 8, 128), up_a, down_a, land_mask, taps, head, sums_a)

    parts = lax.all_to_all(jnp.broadcast_to(partial[:1].reshape(1, 1, 128), (128, 1, 128)), ("lat", "grp"), 0, 0, tiled=True)
    scores, slot = call(
        weight_kernel, (f32(1, 32), f32(1, 32)), in_specs=[SCALAR] + [WHOLE] * 3, out_specs=(WHOLE, WHOLE), name="weights"
    )(me, parts.reshape(128, 128), counts2, source2)
    return new_fields.reshape(32, 30, 8, 128), scores.reshape(32), slot.reshape(32)


def solution(mesh):
    return jax.shard_map(
        local,
        mesh=mesh,
        in_specs=(
            P("grp", None, "lat", None),
            P("lat", None),
            P(),
            P(None, "lat", None),
            P("lat", None),
            P(),
            P(None, "lat", None),
            P(),
            P(),
        ),
        out_specs=(P("grp", None, "lat", None), P("grp"), P("grp")),
        check_vma=False,
    )
```

```python
import functools

import jax
import jax.numpy as jnp
import numpy as np
from jax import lax
from jax.experimental import pallas as pl
from jax.experimental.pallas import tpu as pltpu
from jax.sharding import PartitionSpec as P


LEV = 10
STEPS = 4
STARTS = (0, 8, 16, 22)
DEEP_A = 4
DEEP_B = 5
NA = 20
NB = 32 - NA
BLK = 4
PARAMS = 160
MID = 2 * NA + 120
SCALE = 0.05**0.5
LAG = 4


VMEM = pltpu.VMEM
ANY = pl.ANY
WHOLE = pl.BlockSpec(memory_space=pltpu.VMEM)
SCALAR = pl.BlockSpec(memory_space=pltpu.SMEM)


def split(value):
    high = value.astype(jnp.bfloat16)
    low = (value - high.astype(jnp.float32)).astype(jnp.bfloat16)
    return high, low


def strided_row(ref, base, row, stride):
    parts = [ref[pl.ds(base + start * stride + row, 8, stride=stride), :] for start in STARTS]
    return jnp.concatenate(parts, 0)


def strided_store(ref, row, value):
    for k, start in enumerate(STARTS):
        ref[pl.ds(start * 8 + row, 8, stride=8), :] = value[8 * k : 8 * k + 8]


def first_rows(depth, up_ref, base_up, own_ref, down_ref, base_down):
    def first_row(row):
        if row < depth:
            return strided_row(up_ref, base_up, row, depth)
        if row < depth + 8:
            return strided_row(own_ref, 0, row - depth, 8)
        return strided_row(down_ref, base_down, row - depth - 8, depth)

    return first_row


def emit_pair(member, step, pair, coef, heat, lefts, depth):
    first_row, state, store_last = member
    row = step + 2 * pair
    last = step == STEPS
    shift = DEEP_B - depth

    def load(at):
        if step == 1:
            return first_row(at)
        return state[step % 2][pl.ds(at * 32, 32), :]

    rows = [load(at) for at in range(row - 1, row + 3)]
    smooth = []
    for i in (0, 1):
        here = rows[i + 1]
        at = row + i + shift
        total = (rows[i] + rows[i + 2]) + (pltpu.roll(here, 1, 1) + pltpu.roll(here, 127, 1))
        keep = coef[0, pl.ds(at * 8, 8), :]
        diff = coef[1, pl.ds(at * 8, 8), :]
        smooth.append(jnp.concatenate([keep] * 4, 0) * here + jnp.concatenate([diff] * 4, 0) * total)
    high, low = split(jnp.concatenate(smooth, 1))
    right = jnp.concatenate([high, high, low], 0)
    mixed = jnp.dot(lefts[0 if step == 1 else 2 if last else 1], right, preferred_element_type=jnp.float32)
    for i in (0, 1):
        at = row + i
        part = mixed[:, 128 * i : 128 * (i + 1)]
        warm = heat[1 if last else 0, pl.ds((at + shift) * 32, 32), :]
        if last:
            store_last(at - depth, part * (1.0 - 0.05 * (part * part)) + warm)
        else:
            state[(step + 1) % 2][pl.ds(at * 32, 32), :] = part * (1.0 - part * part) + warm


def run_members(members, coef, heat, lefts, depth):
    count = {step: depth + 4 - step for step in range(1, STEPS + 1)}
    for wave in range(count[1] + LAG * (STEPS - 1) + 1):
        for step in range(1, STEPS + 1):
            pair = wave - LAG * (step - 1)
            if 0 <= pair < count[step]:
                for member in members:
                    emit_pair(member, step, pair, coef, heat, lefts, depth)


def prepare(pup_ref, pdown_ref, hown_ref, diff_ref, mix_ref, coef, heat, lefts):
    for row in range(18):
        if row < 5:
            value = strided_row(pup_ref, 0, row, 5)
            diff = pup_ref[pl.ds(150 + row, 1), :]
        elif row < 13:
            value = strided_row(hown_ref, 0, row - 5, 8)
            diff = diff_ref[pl.ds(row - 5, 1), :]
        else:
            value = strided_row(pdown_ref, 0, row - 13, 5)
            diff = pdown_ref[pl.ds(150 + row - 13, 1), :]
        heat[1, pl.ds(row * 32, 32), :] = value
        heat[0, pl.ds(row * 32, 32), :] = SCALE * value
        diff = jnp.broadcast_to(diff, (8, 128))
        coef[1, pl.ds(row * 8, 8), :] = diff
        coef[0, pl.ds(row * 8, 8), :] = 1.0 - 4.0 * diff
    mix = mix_ref[...]
    for i, factor in enumerate((SCALE, 1.0, 1.0 / SCALE)):
        high, low = split(factor * mix)
        lefts[i] = jnp.concatenate([high, low, high], 1)


def keep_scored(tq_ref, j, out):
    tq_ref[j, 0:8, :] = out[0:8, :]
    tq_ref[j, 8:16, :] = out[8 * LEV : 8 * LEV + 8, :]


def chunk_a_kernel(
    f_ref, up_ref, down_ref, pup_ref, pdown_ref, hown_ref, diff_ref, mix_ref, out_ref, tq_ref, coef, heat, lefts, *states
):
    @pl.when(pl.program_id(0) == 0)
    def _():
        prepare(pup_ref, pdown_ref, hown_ref, diff_ref, mix_ref, coef, heat, lefts)

    def one(p, carry):
        members = []
        for q in range(2):
            j = p * 2 + q
            base = pl.multiple_of(j * 120, 8)
            rows = first_rows(DEEP_A, up_ref, base, f_ref.at[j], down_ref, base)
            members.append((rows, states[2 * q : 2 * q + 2], functools.partial(strided_store, out_ref.at[j])))
        run_members(members, coef, heat, lefts, DEEP_A)
        for q in range(2):
            keep_scored(tq_ref, p * 2 + q, out_ref.at[p * 2 + q])
        return carry

    lax.fori_loop(0, BLK // 2, one, 0)


def chunk_b_kernel(
    f_ref, up_ref, down_ref, pup_ref, pdown_ref, hown_ref, diff_ref, mix_ref, prev_ref, out_ref, tq_ref, edge_ref, coef, heat, lefts,
    *states,
):
    @pl.when(pl.program_id(0) == 0)
    def _():
        prepare(pup_ref, pdown_ref, hown_ref, diff_ref, mix_ref, coef, heat, lefts)

    def store_last(j, row, value):
        if 0 <= row < 8:
            strided_store(out_ref.at[j], row, value)
            return
        slot = 0 if row < 0 else 3
        t, q = value[0:1], value[LEV : LEV + 1]
        edge_ref[j, slot : slot + 1, :] = t
        edge_ref[j, slot + 1 : slot + 2, :] = q
        edge_ref[j, slot + 2 : slot + 3, :] = t

    def one(p, carry):
        members = []
        for q in range(2):
            j = p * 2 + q
            base = j * (30 * DEEP_B)
            rows = first_rows(DEEP_B, up_ref, base, f_ref.at[j], down_ref, base)
            edge_ref[j] = jnp.zeros((8, 128), jnp.float32)
            members.append((rows, states[2 * q : 2 * q + 2], functools.partial(store_last, j)))
        run_members(members, coef, heat, lefts, DEEP_B)
        for q in range(2):
            keep_scored(tq_ref, p * 2 + q, out_ref.at[p * 2 + q])
        return carry

    lax.fori_loop(0, BLK // 2, one, 0)


def send_rows(x_ref, up_ref, down_ref, base, depth):
    for row in range(depth):
        for start in STARTS:
            to = pl.ds(base + start * depth + row, 8, stride=depth)
            down_ref[to, :] = x_ref[pl.ds(start * 8 + row, 8, stride=8), :]
            up_ref[to, :] = x_ref[pl.ds(start * 8 + 8 - depth + row, 8, stride=8), :]


def send_members(f_ref, first, count, depth, up_ref, down_ref, buf, up_buf, down_buf, sems, before):
    rows = BLK * 30 * depth
    blocks = count // BLK
    fetches = [
        pltpu.make_async_copy(f_ref.at[pl.ds(first + k * BLK, BLK)], buf.at[pl.ds(k * BLK, BLK)], sems.at[k]) for k in range(blocks)
    ]
    for fetch in fetches:
        fetch.start()
    copies = []

    def put(start, size, k):
        for i, (source, target) in enumerate(((up_buf, up_ref), (down_buf, down_ref))):
            where = pl.ds(start, size)
            copies.append(pltpu.make_async_copy(source.at[where], target.at[where], sems.at[blocks + 2 * k + i]))
            copies[-1].start()

    extra = before()
    if extra:
        put(count * 30 * depth, extra, blocks)
    for k, fetch in enumerate(fetches):
        fetch.wait()

        def one(j, carry):
            m = k * BLK + j
            send_rows(buf.at[m], up_buf, down_buf, m * (30 * depth), depth)
            return carry

        lax.fori_loop(0, BLK, one, 0)
        put(k * rows, rows, k)
    for copy in copies:
        copy.wait()


def edges_a_kernel(
    me_ref, counts_ref, f_ref, heat_ref, diff_ref, land_ref, pieces_ref, up_ref, down_ref, buf, up_buf, down_buf, sems, hot_sem
):
    me = me_ref[0]
    hot = lax.fori_loop(0, 32, lambda j, at: jnp.where(counts_ref[me * 32 + j] >= 2, j, at), 0)
    fetch = pltpu.make_async_copy(f_ref.at[hot], pieces_ref.at[pl.ds(0, 240)], hot_sem)
    fetch.start()

    def before():
        pieces_ref[240:256, :] = jnp.zeros((16, 128), jnp.float32)
        base = NA * 120
        send_rows(heat_ref, up_buf, down_buf, base, 5)
        diff = diff_ref[...]
        land = land_ref[...].astype(jnp.float32)
        up_buf[base + 150 : base + 155, :] = diff[3:]
        up_buf[base + 155 : base + 160, :] = land[3:]
        down_buf[base + 150 : base + 155, :] = diff[:5]
        down_buf[base + 155 : base + 160, :] = land[:5]
        return PARAMS

    send_members(f_ref, 0, NA, DEEP_A, up_ref, down_ref, buf, up_buf, down_buf, sems, before)
    fetch.wait()


def edges_b_kernel(f_ref, up_ref, down_ref, buf, up_buf, down_buf, sems):
    send_members(f_ref, NA, NB, DEEP_B, up_ref, down_ref, buf, up_buf, down_buf, sems, lambda: 0)


def mid_kernel(donor_ref, tq_ref, up_ref, down_ref):
    for k in range(2 * NA // 8):
        up_ref[pl.ds(8 * k, 8), :] = tq_ref[pl.ds(64 * k + 7, 8, stride=8), :]
        down_ref[pl.ds(8 * k, 8), :] = tq_ref[pl.ds(64 * k, 8, stride=8), :]
    send_rows(donor_ref, up_ref, down_ref, 2 * NA, DEEP_A)


def pick_kernel(index_ref, pieces_ref, out_ref):
    for g in range(16):
        out_ref[g] = pieces_ref[index_ref[g]]


def edge_mask(pup_ref, pdown_ref):
    before, after = pup_ref[159:160, :], pdown_ref[155:156, :]
    one = jnp.ones((1, 128), jnp.float32)
    return jnp.concatenate([before, one, 1.0 - before, after, one, 1.0 - after, one, one], 0)


def score_members(count, tq_ref, edge_ref, land, mask, left, head_ref, acc, first):
    sea = 1.0 - land

    def four(p, carry):
        rights = []
        for pair in range(2):
            cols = []
            for q in range(2):
                m = p * 4 + pair * 2 + q
                t = tq_ref[m, 0:8, :]
                edge = edge_ref[pl.ds(pl.multiple_of(m * 8, 8), 8), :]
                value = jnp.concatenate([t * land, tq_ref[m, 8:16, :], t * sea, edge * mask], 0)
                cols.append(jnp.concatenate([pltpu.roll(value, 1, 1), value, pltpu.roll(value, 127, 1)], 0))
            h, l = split(jnp.concatenate(cols, 1))
            rights.append(jnp.concatenate([h, h, l], 0))
        for pair in range(2):
            total = [jnp.zeros((8, 128), jnp.float32)] * 2
            for block in range(4):
                rows = slice(64 * block, 64 * block + 64)
                hidden = jnp.maximum(jnp.dot(left[rows, :], rights[pair], preferred_element_type=jnp.float32), 0.0)
                head = head_ref[rows, :]
                for q in range(2):
                    part = (hidden[:, 128 * q : 128 * (q + 1)] * head).reshape(8, 8, 128)
                    total[q] = total[q] + jnp.sum(part, 0)
            for q in range(2):
                acc[pl.ds(first + p * 4 + pair * 2 + q, 1), :] = jnp.sum(total[q], 0, keepdims=True)
        return carry

    lax.fori_loop(0, count // 4, four, 0)


def finish_kernel(
    killed_ref, tqa_ref, before_ref, after_ref, tqb_ref, edgeb_ref, land_ref, weight_ref, head_ref, donor_ref,
    pup_ref, pdown_ref, hown_ref, diff_ref, mix_ref, prev_ref,
    out_ref, sums_ref, coef, heat, lefts, s0, s1, donor, edge, left, acc, sems,
):
    prepare(pup_ref, pdown_ref, hown_ref, diff_ref, mix_ref, coef, heat, lefts)
    rows = first_rows(DEEP_A, before_ref, 2 * NA, donor_ref, after_ref, 2 * NA)
    run_members([(rows, (s0, s1), functools.partial(strided_store, donor))], coef, heat, lefts, DEEP_A)

    def copy(m):
        return pltpu.make_async_copy(donor, out_ref.at[m], sems.at[m])

    for m in range(32):
        @pl.when(killed_ref[m] > 0)
        def _():
            copy(m).start()

    zero = jnp.zeros((8, 128), jnp.float32)
    for k in range((NA + 7) // 8):
        parts = [ref[pl.ds(16 * k + i, 8, stride=2), :] for ref in (before_ref, after_ref) for i in (0, 1)]
        for slot, value in enumerate((parts[0], parts[1], parts[0], parts[2], parts[3], parts[2], zero, zero)):
            edge[pl.ds(64 * k + slot, 8, stride=8), :] = value
    high, low = split(weight_ref[...])
    left[...] = jnp.concatenate([high, low, high], 1)
    land = land_ref[...].astype(jnp.float32)
    mask = edge_mask(pup_ref, pdown_ref)
    score_members(NA, tqa_ref, edge, land, mask, left, head_ref, acc, 0)
    score_members(NB, tqb_ref, edgeb_ref, land, mask, left, head_ref, acc, NA)
    ones = jnp.ones((8, 128), jnp.float32)
    padded = jnp.concatenate([acc[...], jnp.zeros((96, 128), jnp.float32)], 0)
    sums = lax.dot_general(
        ones, padded, (((1,), (1,)), ((), ())), precision=lax.Precision.HIGHEST, preferred_element_type=jnp.float32
    )
    for k in range(16):
        sums_ref[pl.ds(8 * k, 8), :] = sums
    for m in range(32):
        @pl.when(killed_ref[m] > 0)
        def _():
            copy(m).wait()


def weight_kernel(me_ref, parts_ref, counts_ref, source_ref, scores_ref, slot_ref):
    me = me_ref[0]
    scores = jnp.sum(parts_ref[...].reshape(8, 16, 128), 0)[:, :32]
    weights = jnp.exp(scores)
    total = jnp.sum(weights)
    weights = weights / (total / 512.0)
    counts = counts_ref[...].astype(jnp.float32)
    group = lax.broadcasted_iota(jnp.int32, (16, 32), 0)
    member = lax.broadcasted_iota(jnp.int32, (16, 32), 1)
    flat = group * 32 + member
    source = source_ref[...]
    mine = group == me
    killed = jnp.logical_and(mine, source != flat)
    donor = jnp.max(jnp.where(killed, source, -1))
    here = flat == donor
    donor_weight = jnp.sum(jnp.where(here, weights, 0.0))
    donor_count = jnp.sum(jnp.where(here, counts, 0.0))
    top = jnp.where(killed, donor_weight, weights)
    under = jnp.where(killed, donor_count, counts)
    share = jnp.where(mine, top / jnp.where(mine, under, 1.0), 0.0)
    own = jnp.where(mine, scores, 0.0)
    scores_ref[...] = jnp.sum(own, 0, keepdims=True)
    slot_ref[...] = jnp.sum(share, 0, keepdims=True)


def spread_matrix():
    table = np.zeros((27, 8, 96), np.float32)
    for k in range(3):
        for a in (-1, 0, 1):
            for b in (-1, 0, 1):
                tap = 9 * k + 3 * (a + 1) + (b + 1)
                for i in range(8):
                    row = i + a
                    if 0 <= row < 8:
                        slot = 8 * k + row
                    elif row < 0:
                        slot = 24 + k
                    else:
                        slot = 27 + k
                    table[tap, i, (b + 1) * 32 + slot] = 1.0
    return table.reshape(27, 8 * 96)


def call(kernel, outs, **kw):
    return pl.pallas_call(kernel, out_shape=outs, **kw)


def f32(*shape):
    return jax.ShapeDtypeStruct(shape, jnp.float32)


def local(fields, diffusion, mixing, heating, land_mask, conv_weight, head_weight, counts, source):
    size = lax.axis_size("lat")
    up = [(i, i + 1) for i in range(size - 1)]
    down = [(i + 1, i) for i in range(size - 1)]
    me = lax.axis_index("grp").reshape(1).astype(jnp.int32)
    counts2 = counts.reshape(16, 32)
    source2 = source.reshape(16, 32)
    f = fields.reshape(32, 240, 128)
    heat = heating.reshape(240, 128)
    hbm = pl.BlockSpec(memory_space=ANY)

    def edge_scratch(count, rows):
        return [
            VMEM((count, 240, 128), jnp.float32),
            VMEM((rows, 128), jnp.float32),
            VMEM((rows, 128), jnp.float32),
            pltpu.SemaphoreType.DMA((3 * (count // BLK) + 2,)),
        ]

    rows_a = NA * 120 + PARAMS
    pieces, send_up_a, send_down_a = call(
        edges_a_kernel,
        (f32(256, 128), f32(rows_a, 128), f32(rows_a, 128)),
        in_specs=[SCALAR, SCALAR, hbm, WHOLE, WHOLE, WHOLE],
        out_specs=(WHOLE, hbm, hbm),
        scratch_shapes=edge_scratch(NA, rows_a) + [pltpu.SemaphoreType.DMA],
        name="edges_a",
    )(me, counts, f, heat, diffusion, land_mask)

    pieces = lax.all_to_all(pieces.reshape(16, 16, 128), "grp", 0, 0, tiled=True)
    up_a = lax.ppermute(send_up_a, "lat", up)
    down_a = lax.ppermute(send_down_a, "lat", down)
    flat = jnp.arange(512, dtype=jnp.int32).reshape(16, 32)
    donor_group = jnp.max(jnp.where(source2 != flat, source2 // 32, 0), 1)
    pieces = call(pick_kernel, f32(16, 16, 128), in_specs=[SCALAR, WHOLE], out_specs=WHOLE, name="pick")(donor_group, pieces)
    donor_state = lax.all_to_all(pieces, "grp", 0, 0, tiled=True).reshape(256, 128)

    send_up_b, send_down_b = call(
        edges_b_kernel,
        (f32(NB * 150, 128), f32(NB * 150, 128)),
        in_specs=[hbm],
        out_specs=(hbm, hbm),
        scratch_shapes=edge_scratch(NB, NB * 150),
        name="edges_b",
    )(f)
    up_b = lax.ppermute(send_up_b, "lat", up)
    down_b = lax.ppermute(send_down_b, "lat", down)

    mix = jnp.concatenate([mixing[:24], mixing[22:]], 0)
    mix = jnp.concatenate([mix[:, :24], jnp.zeros((32, 2), jnp.float32), mix[:, 24:]], 1)
    taps = jnp.dot(conv_weight, jnp.asarray(spread_matrix()), precision=lax.Precision.HIGHEST).reshape(256, 96)
    head = head_weight.reshape(256, 128)
    killed = (lax.dynamic_index_in_dim(counts2, me[0], 0, keepdims=False) == 0).astype(jnp.int32)

    def whole(shape, at=0):
        return pl.BlockSpec(shape, lambda *i: (at,) + (0,) * (len(shape) - 1))

    params = whole((PARAMS, 128), NA * 120 // PARAMS)
    block = pl.BlockSpec((BLK, 240, 128), lambda i: (i, 0, 0))
    tq_block = pl.BlockSpec((BLK, 16, 128), lambda i: (i, 0, 0))
    step_scratch = [
        VMEM((2, 18 * 8, 128), jnp.float32),
        VMEM((2, 18 * 32, 128), jnp.float32),
        VMEM((3, 32, 96), jnp.bfloat16),
    ] + [VMEM((18 * 32, 128), jnp.float32)] * 4
    shared = [params, params, WHOLE, WHOLE, WHOLE]
    halo_a = pl.BlockSpec((BLK * 30 * DEEP_A, 128), lambda i: (i, 0))
    state_a, tq_a = call(
        chunk_a_kernel,
        (f32(32, 240, 128), f32(NA, 16, 128)),
        grid=(NA // BLK,),
        in_specs=[block, halo_a, halo_a] + shared,
        out_specs=(block, tq_block),
        scratch_shapes=step_scratch,
        name="chunk_a",
    )(f, up_a, down_a, up_a, down_a, heat, diffusion, mix)

    send_up, send_down = call(
        mid_kernel, (f32(MID, 128), f32(MID, 128)), in_specs=[WHOLE, WHOLE], out_specs=(WHOLE, WHOLE), name="mid"
    )(donor_state, tq_a.reshape(NA * 16, 128))
    before = lax.ppermute(send_up, "lat", up)
    after = lax.ppermute(send_down, "lat", down)

    halo_b = pl.BlockSpec((BLK * 30 * DEEP_B, 128), lambda i: (i, 0))
    block_b = pl.BlockSpec((BLK, 240, 128), lambda i: (i + NA // BLK, 0, 0))
    state_b, tq_b, edge_b = call(
        chunk_b_kernel,
        (f32(32, 240, 128), f32(NB, 16, 128), f32(NB, 8, 128)),
        grid=(NB // BLK,),
        in_specs=[block_b, halo_b, halo_b] + shared + [hbm],
        out_specs=(block_b, tq_block, pl.BlockSpec((BLK, 8, 128), lambda i: (i, 0, 0))),
        scratch_shapes=step_scratch,
        input_output_aliases={8: 0},
        name="chunk_b",
    )(f, up_b, down_b, up_a, down_a, heat, diffusion, mix, state_a)

    new_fields, sums = call(
        finish_kernel,
        (f32(32, 240, 128), f32(128, 128)),
        grid=(1,),
        in_specs=[SCALAR] + [WHOLE] * 9 + shared + [hbm],
        out_specs=(hbm, WHOLE),
        scratch_shapes=step_scratch[:-2]
        + [
            VMEM((240, 128), jnp.float32),
            VMEM(((NA + 7) // 8 * 64, 128), jnp.float32),
            VMEM((256, 288), jnp.bfloat16),
            VMEM((32, 128), jnp.float32),
            pltpu.SemaphoreType.DMA((32,)),
        ],
        input_output_aliases={15: 0},
        name="finish",
    )(
        killed, tq_a, before, after, tq_b, edge_b.reshape(NB * 8, 128), land_mask, taps, head, donor_state,
        up_a, down_a, heat, diffusion, mix, state_b,
    )

    parts = lax.all_to_all(sums.reshape(128, 1, 128), ("lat", "grp"), 0, 0, tiled=True)
    scores, slot = call(
        weight_kernel, (f32(1, 32), f32(1, 32)), in_specs=[SCALAR] + [WHOLE] * 3, out_specs=(WHOLE, WHOLE), name="weights"
    )(me, parts.reshape(128, 128), counts2, source2)
    return new_fields.reshape(32, 30, 8, 128), scores.reshape(32), slot.reshape(32)


def solution(mesh):
    return jax.shard_map(
        local,
        mesh=mesh,
        in_specs=(
            P("grp", None, "lat", None),
            P("lat", None),
            P(),
            P(None, "lat", None),
            P("lat", None),
            P(),
            P(None, "lat", None),
            P(),
            P(),
        ),
        out_specs=(P("grp", None, "lat", None), P("grp"), P("grp")),
        check_vma=False,
    )
```

```python
import functools

import jax
import jax.numpy as jnp
import numpy as np
from jax import lax
from jax.experimental import pallas as pl
from jax.experimental.pallas import tpu as pltpu
from jax.sharding import PartitionSpec as P


LEV = 10
STEPS = 4
STARTS = (0, 8, 16, 22)
DEEP_A = 4
DEEP_B = 5
NA = 20
NB = 32 - NA
BLK = 4
PARAMS = 160
MID = 2 * NA + 120
SCALE = 0.05**0.5
LAG = 4


VMEM = pltpu.VMEM
ANY = pl.ANY
WHOLE = pl.BlockSpec(memory_space=pltpu.VMEM)
SCALAR = pl.BlockSpec(memory_space=pltpu.SMEM)


def split(value):
    high = value.astype(jnp.bfloat16)
    low = (value - high.astype(jnp.float32)).astype(jnp.bfloat16)
    return high, low


def strided_row(ref, base, row, stride):
    parts = [ref[pl.ds(base + start * stride + row, 8, stride=stride), :] for start in STARTS]
    return jnp.concatenate(parts, 0)


def strided_store(ref, row, value):
    for k, start in enumerate(STARTS):
        ref[pl.ds(start * 8 + row, 8, stride=8), :] = value[8 * k : 8 * k + 8]


def first_rows(depth, up_ref, base_up, own_ref, down_ref, base_down):
    def first_row(row):
        if row < depth:
            return strided_row(up_ref, base_up, row, depth)
        if row < depth + 8:
            return strided_row(own_ref, 0, row - depth, 8)
        return strided_row(down_ref, base_down, row - depth - 8, depth)

    return first_row


def emit_pair(member, step, pair, coef, heat, lefts, depth):
    first_row, state, store_last = member
    row = step + 2 * pair
    last = step == STEPS
    shift = DEEP_B - depth

    def load(at):
        if step == 1:
            return first_row(at)
        return state[step % 2][pl.ds(at * 32, 32), :]

    rows = [load(at) for at in range(row - 1, row + 3)]
    smooth = []
    for i in (0, 1):
        here = rows[i + 1]
        at = row + i + shift
        total = (rows[i] + rows[i + 2]) + (pltpu.roll(here, 1, 1) + pltpu.roll(here, 127, 1))
        keep = coef[0, pl.ds(at * 8, 8), :]
        diff = coef[1, pl.ds(at * 8, 8), :]
        smooth.append(jnp.concatenate([keep] * 4, 0) * here + jnp.concatenate([diff] * 4, 0) * total)
    high, low = split(jnp.concatenate(smooth, 1))
    right = jnp.concatenate([high, high, low], 0)
    mixed = jnp.dot(lefts[0 if step == 1 else 2 if last else 1], right, preferred_element_type=jnp.float32)
    for i in (0, 1):
        at = row + i
        part = mixed[:, 128 * i : 128 * (i + 1)]
        warm = heat[1 if last else 0, pl.ds((at + shift) * 32, 32), :]
        if last:
            store_last(at - depth, part * (1.0 - 0.05 * (part * part)) + warm)
        else:
            state[(step + 1) % 2][pl.ds(at * 32, 32), :] = part * (1.0 - part * part) + warm


def run_members(members, coef, heat, lefts, depth):
    count = {step: depth + 4 - step for step in range(1, STEPS + 1)}
    for wave in range(count[1] + LAG * (STEPS - 1) + 1):
        for step in range(1, STEPS + 1):
            pair = wave - LAG * (step - 1)
            if 0 <= pair < count[step]:
                for member in members:
                    emit_pair(member, step, pair, coef, heat, lefts, depth)


def prepare(pup_ref, pdown_ref, hown_ref, diff_ref, mix_ref, coef, heat, lefts):
    for row in range(18):
        if row < 5:
            value = strided_row(pup_ref, 0, row, 5)
            diff = pup_ref[pl.ds(150 + row, 1), :]
        elif row < 13:
            value = strided_row(hown_ref, 0, row - 5, 8)
            diff = diff_ref[pl.ds(row - 5, 1), :]
        else:
            value = strided_row(pdown_ref, 0, row - 13, 5)
            diff = pdown_ref[pl.ds(150 + row - 13, 1), :]
        heat[1, pl.ds(row * 32, 32), :] = value
        heat[0, pl.ds(row * 32, 32), :] = SCALE * value
        diff = jnp.broadcast_to(diff, (8, 128))
        coef[1, pl.ds(row * 8, 8), :] = diff
        coef[0, pl.ds(row * 8, 8), :] = 1.0 - 4.0 * diff
    mix = mix_ref[...]
    for i, factor in enumerate((SCALE, 1.0, 1.0 / SCALE)):
        high, low = split(factor * mix)
        lefts[i] = jnp.concatenate([high, low, high], 1)


def keep_scored(tq_ref, j, out):
    tq_ref[j, 0:8, :] = out[0:8, :]
    tq_ref[j, 8:16, :] = out[8 * LEV : 8 * LEV + 8, :]


def chunk_a_kernel(
    f_ref, up_ref, down_ref, pup_ref, pdown_ref, hown_ref, diff_ref, mix_ref, out_ref, tq_ref, pup_out, pdown_out, coef, heat, lefts,
    *states,
):
    @pl.when(pl.program_id(0) == 0)
    def _():
        prepare(pup_ref, pdown_ref, hown_ref, diff_ref, mix_ref, coef, heat, lefts)
        pup_out[...] = pup_ref[...]
        pdown_out[...] = pdown_ref[...]

    def one(p, carry):
        members = []
        for q in range(2):
            j = p * 2 + q
            base = pl.multiple_of(j * 120, 8)
            rows = first_rows(DEEP_A, up_ref, base, f_ref.at[j], down_ref, base)
            members.append((rows, states[2 * q : 2 * q + 2], functools.partial(strided_store, out_ref.at[j])))
        run_members(members, coef, heat, lefts, DEEP_A)
        for q in range(2):
            keep_scored(tq_ref, p * 2 + q, out_ref.at[p * 2 + q])
        return carry

    lax.fori_loop(0, BLK // 2, one, 0)


def chunk_b_kernel(
    f_ref, up_ref, down_ref, pup_ref, pdown_ref, hown_ref, diff_ref, mix_ref, prev_ref, out_ref, tq_ref, edge_ref, coef, heat, lefts,
    *states,
):
    @pl.when(pl.program_id(0) == 0)
    def _():
        prepare(pup_ref, pdown_ref, hown_ref, diff_ref, mix_ref, coef, heat, lefts)

    def store_last(j, row, value):
        if 0 <= row < 8:
            strided_store(out_ref.at[j], row, value)
            return
        slot = 0 if row < 0 else 3
        t, q = value[0:1], value[LEV : LEV + 1]
        edge_ref[j, slot : slot + 1, :] = t
        edge_ref[j, slot + 1 : slot + 2, :] = q
        edge_ref[j, slot + 2 : slot + 3, :] = t

    def one(p, carry):
        members = []
        for q in range(2):
            j = p * 2 + q
            base = j * (30 * DEEP_B)
            rows = first_rows(DEEP_B, up_ref, base, f_ref.at[j], down_ref, base)
            edge_ref[j] = jnp.zeros((8, 128), jnp.float32)
            members.append((rows, states[2 * q : 2 * q + 2], functools.partial(store_last, j)))
        run_members(members, coef, heat, lefts, DEEP_B)
        for q in range(2):
            keep_scored(tq_ref, p * 2 + q, out_ref.at[p * 2 + q])
        return carry

    lax.fori_loop(0, BLK // 2, one, 0)


def send_rows(x_ref, up_ref, down_ref, base, depth):
    for row in range(depth):
        for start in STARTS:
            to = pl.ds(base + start * depth + row, 8, stride=depth)
            down_ref[to, :] = x_ref[pl.ds(start * 8 + row, 8, stride=8), :]
            up_ref[to, :] = x_ref[pl.ds(start * 8 + 8 - depth + row, 8, stride=8), :]


def send_members(f_ref, first, count, depth, up_ref, down_ref, buf, up_buf, down_buf, sems, before):
    rows = BLK * 30 * depth
    blocks = count // BLK
    fetches = [
        pltpu.make_async_copy(f_ref.at[pl.ds(first + k * BLK, BLK)], buf.at[pl.ds(k * BLK, BLK)], sems.at[k]) for k in range(blocks)
    ]
    for fetch in fetches:
        fetch.start()
    copies = []

    def put(start, size, k):
        for i, (source, target) in enumerate(((up_buf, up_ref), (down_buf, down_ref))):
            where = pl.ds(start, size)
            copies.append(pltpu.make_async_copy(source.at[where], target.at[where], sems.at[blocks + 2 * k + i]))
            copies[-1].start()

    extra = before()
    if extra:
        put(count * 30 * depth, extra, blocks)
    for k, fetch in enumerate(fetches):
        fetch.wait()

        def one(j, carry):
            m = k * BLK + j
            send_rows(buf.at[m], up_buf, down_buf, m * (30 * depth), depth)
            return carry

        lax.fori_loop(0, BLK, one, 0)
        put(k * rows, rows, k)
    for copy in copies:
        copy.wait()


def edges_a_kernel(
    me_ref, counts_ref, f_ref, heat_ref, diff_ref, land_ref, pieces_ref, up_ref, down_ref, buf, up_buf, down_buf, sems, pieces, hot_sems
):
    put_pieces = pltpu.make_async_copy(pieces, pieces_ref, hot_sems.at[1])

    def before():
        base = me_ref[0] * 32
        hot = jnp.int32(0)
        for j in range(1, 32):
            hot = jnp.where(counts_ref[base + j] >= 2, j, hot)
        fetch = pltpu.make_async_copy(f_ref.at[hot], pieces.at[pl.ds(0, 240)], hot_sems.at[0])
        fetch.start()
        pieces[240:256, :] = jnp.zeros((16, 128), jnp.float32)
        base = NA * 120
        send_rows(heat_ref, up_buf, down_buf, base, 5)
        diff = diff_ref[...]
        land = land_ref[...].astype(jnp.float32)
        up_buf[base + 150 : base + 155, :] = diff[3:]
        up_buf[base + 155 : base + 160, :] = land[3:]
        down_buf[base + 150 : base + 155, :] = diff[:5]
        down_buf[base + 155 : base + 160, :] = land[:5]
        fetch.wait()
        put_pieces.start()
        return PARAMS

    send_members(f_ref, 0, NA, DEEP_A, up_ref, down_ref, buf, up_buf, down_buf, sems, before)
    put_pieces.wait()


def edges_b_kernel(f_ref, up_ref, down_ref, buf, up_buf, down_buf, sems):
    send_members(f_ref, NA, NB, DEEP_B, up_ref, down_ref, buf, up_buf, down_buf, sems, lambda: 0)


def mid_kernel(donor_ref, tq_ref, up_ref, down_ref):
    for k in range(2 * NA // 8):
        up_ref[pl.ds(8 * k, 8), :] = tq_ref[pl.ds(64 * k + 7, 8, stride=8), :]
        down_ref[pl.ds(8 * k, 8), :] = tq_ref[pl.ds(64 * k, 8, stride=8), :]
    send_rows(donor_ref, up_ref, down_ref, 2 * NA, DEEP_A)


def pick_kernel(index_ref, pieces_ref, out_ref):
    for g in range(16):
        out_ref[g] = pieces_ref[index_ref[g]]


def edge_mask(pup_ref, pdown_ref):
    before, after = pup_ref[159:160, :], pdown_ref[155:156, :]
    one = jnp.ones((1, 128), jnp.float32)
    return jnp.concatenate([before, one, 1.0 - before, after, one, 1.0 - after, one, one], 0)


def score_members(count, tq_ref, edge_ref, land, mask, left, head_ref, acc, first):
    sea = 1.0 - land

    def four(p, carry):
        rights = []
        for pair in range(2):
            cols = []
            for q in range(2):
                m = p * 4 + pair * 2 + q
                t = tq_ref[m, 0:8, :]
                edge = edge_ref[pl.ds(pl.multiple_of(m * 8, 8), 8), :]
                value = jnp.concatenate([t * land, tq_ref[m, 8:16, :], t * sea, edge * mask], 0)
                cols.append(jnp.concatenate([pltpu.roll(value, 1, 1), value, pltpu.roll(value, 127, 1)], 0))
            h, l = split(jnp.concatenate(cols, 1))
            rights.append(jnp.concatenate([h, h, l], 0))
        for pair in range(2):
            total = [jnp.zeros((8, 128), jnp.float32)] * 2
            for block in range(4):
                rows = slice(64 * block, 64 * block + 64)
                hidden = jnp.maximum(jnp.dot(left[rows, :], rights[pair], preferred_element_type=jnp.float32), 0.0)
                head = head_ref[rows, :]
                for q in range(2):
                    part = (hidden[:, 128 * q : 128 * (q + 1)] * head).reshape(8, 8, 128)
                    total[q] = total[q] + jnp.sum(part, 0)
            for q in range(2):
                acc[pl.ds(first + p * 4 + pair * 2 + q, 1), :] = jnp.sum(total[q], 0, keepdims=True)
        return carry

    lax.fori_loop(0, count // 4, four, 0)


def finish_kernel(
    killed_ref, tqa_ref, before_ref, after_ref, tqb_ref, edgeb_ref, land_ref, weight_ref, head_ref, donor_ref,
    pup_ref, pdown_ref, hown_ref, diff_ref, mix_ref, prev_ref,
    out_ref, sums_ref, coef, heat, lefts, s0, s1, donor, edge, left, acc, sems,
):
    prepare(pup_ref, pdown_ref, hown_ref, diff_ref, mix_ref, coef, heat, lefts)
    rows = first_rows(DEEP_A, before_ref, 2 * NA, donor_ref, after_ref, 2 * NA)
    run_members([(rows, (s0, s1), functools.partial(strided_store, donor))], coef, heat, lefts, DEEP_A)

    def copy(m):
        return pltpu.make_async_copy(donor, out_ref.at[m], sems.at[m])

    for m in range(32):
        @pl.when(killed_ref[m] > 0)
        def _():
            copy(m).start()

    zero = jnp.zeros((8, 128), jnp.float32)
    for k in range((NA + 7) // 8):
        parts = [ref[pl.ds(16 * k + i, 8, stride=2), :] for ref in (before_ref, after_ref) for i in (0, 1)]
        for slot, value in enumerate((parts[0], parts[1], parts[0], parts[2], parts[3], parts[2], zero, zero)):
            edge[pl.ds(64 * k + slot, 8, stride=8), :] = value
    high, low = split(weight_ref[...])
    left[...] = jnp.concatenate([high, low, high], 1)
    land = land_ref[...].astype(jnp.float32)
    mask = edge_mask(pup_ref, pdown_ref)
    score_members(NA, tqa_ref, edge, land, mask, left, head_ref, acc, 0)
    score_members(NB, tqb_ref, edgeb_ref, land, mask, left, head_ref, acc, NA)
    ones = jnp.ones((8, 128), jnp.float32)
    padded = jnp.concatenate([acc[...], jnp.zeros((96, 128), jnp.float32)], 0)
    sums = lax.dot_general(
        ones, padded, (((1,), (1,)), ((), ())), precision=lax.Precision.HIGHEST, preferred_element_type=jnp.float32
    )
    for k in range(16):
        sums_ref[pl.ds(8 * k, 8), :] = sums
    for m in range(32):
        @pl.when(killed_ref[m] > 0)
        def _():
            copy(m).wait()


def weight_kernel(me_ref, parts_ref, counts_ref, source_ref, scores_ref, slot_ref):
    me = me_ref[0]
    scores = jnp.sum(parts_ref[...].reshape(8, 16, 128), 0)[:, :32]
    weights = jnp.exp(scores)
    total = jnp.sum(weights)
    weights = weights / (total / 512.0)
    counts = counts_ref[...].astype(jnp.float32)
    group = lax.broadcasted_iota(jnp.int32, (16, 32), 0)
    member = lax.broadcasted_iota(jnp.int32, (16, 32), 1)
    flat = group * 32 + member
    source = source_ref[...]
    mine = group == me
    killed = jnp.logical_and(mine, source != flat)
    donor = jnp.max(jnp.where(killed, source, -1))
    here = flat == donor
    donor_weight = jnp.sum(jnp.where(here, weights, 0.0))
    donor_count = jnp.sum(jnp.where(here, counts, 0.0))
    top = jnp.where(killed, donor_weight, weights)
    under = jnp.where(killed, donor_count, counts)
    share = jnp.where(mine, top / jnp.where(mine, under, 1.0), 0.0)
    own = jnp.where(mine, scores, 0.0)
    scores_ref[...] = jnp.sum(own, 0, keepdims=True)
    slot_ref[...] = jnp.sum(share, 0, keepdims=True)


def spread_matrix():
    table = np.zeros((27, 8, 96), np.float32)
    for k in range(3):
        for a in (-1, 0, 1):
            for b in (-1, 0, 1):
                tap = 9 * k + 3 * (a + 1) + (b + 1)
                for i in range(8):
                    row = i + a
                    if 0 <= row < 8:
                        slot = 8 * k + row
                    elif row < 0:
                        slot = 24 + k
                    else:
                        slot = 27 + k
                    table[tap, i, (b + 1) * 32 + slot] = 1.0
    return table.reshape(27, 8 * 96)


GRANT = {"chunk_a": 50, "chunk_b": 53, "pick": 24, "mid": 24, "finish": 24, "weights": 24}


def call(kernel, outs, name, **kw):
    params = pltpu.CompilerParams(vmem_limit_bytes=GRANT[name] << 20) if name in GRANT else None
    return pl.pallas_call(kernel, out_shape=outs, compiler_params=params, **kw)


def f32(*shape):
    return jax.ShapeDtypeStruct(shape, jnp.float32)


def local(fields, diffusion, mixing, heating, land_mask, conv_weight, head_weight, counts, source):
    size = lax.axis_size("lat")
    up = [(i, i + 1) for i in range(size - 1)]
    down = [(i + 1, i) for i in range(size - 1)]
    me = lax.axis_index("grp").reshape(1).astype(jnp.int32)
    counts2 = counts.reshape(16, 32)
    source2 = source.reshape(16, 32)
    f = fields.reshape(32, 240, 128)
    heat = heating.reshape(240, 128)
    hbm = pl.BlockSpec(memory_space=ANY)

    def edge_scratch(count, rows):
        return [
            VMEM((count, 240, 128), jnp.float32),
            VMEM((rows, 128), jnp.float32),
            VMEM((rows, 128), jnp.float32),
            pltpu.SemaphoreType.DMA((3 * (count // BLK) + 2,)),
        ]

    rows_a = NA * 120 + PARAMS
    pieces, send_up_a, send_down_a = call(
        edges_a_kernel,
        (f32(256, 128), f32(rows_a, 128), f32(rows_a, 128)),
        in_specs=[SCALAR, SCALAR, hbm, WHOLE, WHOLE, WHOLE],
        out_specs=(hbm, hbm, hbm),
        scratch_shapes=edge_scratch(NA, rows_a) + [VMEM((256, 128), jnp.float32), pltpu.SemaphoreType.DMA((2,))],
        name="edges_a",
    )(me, counts, f, heat, diffusion, land_mask)

    pieces = lax.all_to_all(pieces.reshape(16, 16, 128), "grp", 0, 0, tiled=True)
    up_a = lax.ppermute(send_up_a, "lat", up)
    down_a = lax.ppermute(send_down_a, "lat", down)
    flat = jnp.arange(512, dtype=jnp.int32).reshape(16, 32)
    donor_group = jnp.max(jnp.where(source2 != flat, source2 // 32, 0), 1)
    pieces = call(pick_kernel, f32(16, 16, 128), in_specs=[SCALAR, WHOLE], out_specs=WHOLE, name="pick")(donor_group, pieces)
    donor_state = lax.all_to_all(pieces, "grp", 0, 0, tiled=True).reshape(256, 128)

    send_up_b, send_down_b = call(
        edges_b_kernel,
        (f32(NB * 150, 128), f32(NB * 150, 128)),
        in_specs=[hbm],
        out_specs=(hbm, hbm),
        scratch_shapes=edge_scratch(NB, NB * 150),
        name="edges_b",
    )(f)
    up_b = lax.ppermute(send_up_b, "lat", up)
    down_b = lax.ppermute(send_down_b, "lat", down)

    mix = jnp.concatenate([mixing[:24], mixing[22:]], 0)
    mix = jnp.concatenate([mix[:, :24], jnp.zeros((32, 2), jnp.float32), mix[:, 24:]], 1)
    taps = jnp.dot(conv_weight, jnp.asarray(spread_matrix()), precision=lax.Precision.HIGHEST).reshape(256, 96)
    head = head_weight.reshape(256, 128)
    killed = (lax.dynamic_index_in_dim(counts2, me[0], 0, keepdims=False) == 0).astype(jnp.int32)

    def whole(shape, at=0):
        return pl.BlockSpec(shape, lambda *i: (at,) + (0,) * (len(shape) - 1))

    params = whole((PARAMS, 128), NA * 120 // PARAMS)
    block = pl.BlockSpec((BLK, 240, 128), lambda i: (i, 0, 0))
    tq_block = pl.BlockSpec((BLK, 16, 128), lambda i: (i, 0, 0))
    step_scratch = [
        VMEM((2, 18 * 8, 128), jnp.float32),
        VMEM((2, 18 * 32, 128), jnp.float32),
        VMEM((3, 32, 96), jnp.bfloat16),
    ] + [VMEM((18 * 32, 128), jnp.float32)] * 4
    shared = [params, params, WHOLE, WHOLE, WHOLE]
    halo_a = pl.BlockSpec((BLK * 30 * DEEP_A, 128), lambda i: (i, 0))
    whole_params = whole((PARAMS, 128))
    state_a, tq_a, params_up, params_down = call(
        chunk_a_kernel,
        (f32(32, 240, 128), f32(NA, 16, 128), f32(PARAMS, 128), f32(PARAMS, 128)),
        grid=(NA // BLK,),
        in_specs=[block, halo_a, halo_a] + shared,
        out_specs=(block, tq_block, whole_params, whole_params),
        scratch_shapes=step_scratch,
        name="chunk_a",
    )(f, up_a, down_a, up_a, down_a, heat, diffusion, mix)

    send_up, send_down = call(
        mid_kernel, (f32(MID, 128), f32(MID, 128)), in_specs=[WHOLE, WHOLE], out_specs=(WHOLE, WHOLE), name="mid"
    )(donor_state, tq_a.reshape(NA * 16, 128))
    before = lax.ppermute(send_up, "lat", up)
    after = lax.ppermute(send_down, "lat", down)

    halo_b = pl.BlockSpec((BLK * 30 * DEEP_B, 128), lambda i: (i, 0))
    block_b = pl.BlockSpec((BLK, 240, 128), lambda i: (i + NA // BLK, 0, 0))
    state_b, tq_b, edge_b = call(
        chunk_b_kernel,
        (f32(32, 240, 128), f32(NB, 16, 128), f32(NB, 8, 128)),
        grid=(NB // BLK,),
        in_specs=[block_b, halo_b, halo_b] + [WHOLE] * 5 + [hbm],
        out_specs=(block_b, tq_block, pl.BlockSpec((BLK, 8, 128), lambda i: (i, 0, 0))),
        scratch_shapes=step_scratch,
        input_output_aliases={8: 0},
        name="chunk_b",
    )(f, up_b, down_b, params_up, params_down, heat, diffusion, mix, state_a)

    new_fields, sums = call(
        finish_kernel,
        (f32(32, 240, 128), f32(128, 128)),
        grid=(1,),
        in_specs=[SCALAR] + [WHOLE] * 14 + [hbm],
        out_specs=(hbm, WHOLE),
        scratch_shapes=step_scratch[:-2]
        + [
            VMEM((240, 128), jnp.float32),
            VMEM(((NA + 7) // 8 * 64, 128), jnp.float32),
            VMEM((256, 288), jnp.bfloat16),
            VMEM((32, 128), jnp.float32),
            pltpu.SemaphoreType.DMA((32,)),
        ],
        input_output_aliases={15: 0},
        name="finish",
    )(
        killed, tq_a, before, after, tq_b, edge_b.reshape(NB * 8, 128), land_mask, taps, head, donor_state,
        params_up, params_down, heat, diffusion, mix, state_b,
    )

    parts = lax.all_to_all(sums.reshape(128, 1, 128), ("lat", "grp"), 0, 0, tiled=True)
    scores, slot = call(
        weight_kernel, (f32(1, 32), f32(1, 32)), in_specs=[SCALAR] + [WHOLE] * 3, out_specs=(WHOLE, WHOLE), name="weights"
    )(me, parts.reshape(128, 128), counts2, source2)
    return new_fields.reshape(32, 30, 8, 128), scores.reshape(32), slot.reshape(32)


def solution(mesh):
    return jax.shard_map(
        local,
        mesh=mesh,
        in_specs=(
            P("grp", None, "lat", None),
            P("lat", None),
            P(),
            P(None, "lat", None),
            P("lat", None),
            P(),
            P(None, "lat", None),
            P(),
            P(),
        ),
        out_specs=(P("grp", None, "lat", None), P("grp"), P("grp")),
        check_vma=False,
    )
```

```python
import functools

import jax
import jax.numpy as jnp
import numpy as np
from jax import lax
from jax.experimental import pallas as pl
from jax.experimental.pallas import tpu as pltpu
from jax.sharding import PartitionSpec as P


LEV = 10
STEPS = 4
STARTS = (0, 8, 16, 22)
DEEP_A = 4
DEEP_B = 5
NA = 20
NB = 32 - NA
BLK = 4
PARAMS = 160
MID = 2 * NA + 120
SCALE = 0.05**0.5
LAG = 4


VMEM = pltpu.VMEM
ANY = pl.ANY
WHOLE = pl.BlockSpec(memory_space=pltpu.VMEM)
SCALAR = pl.BlockSpec(memory_space=pltpu.SMEM)


def split(value):
    high = value.astype(jnp.bfloat16)
    low = (value - high.astype(jnp.float32)).astype(jnp.bfloat16)
    return high, low


def strided_row(ref, base, row, stride):
    parts = [ref[pl.ds(base + start * stride + row, 8, stride=stride), :] for start in STARTS]
    return jnp.concatenate(parts, 0)


def strided_store(ref, row, value):
    for k, start in enumerate(STARTS):
        ref[pl.ds(start * 8 + row, 8, stride=8), :] = value[8 * k : 8 * k + 8]


def first_rows(depth, up_ref, base_up, own_ref, down_ref, base_down):
    def first_row(row):
        if row < depth:
            return strided_row(up_ref, base_up, row, depth)
        if row < depth + 8:
            return strided_row(own_ref, 0, row - depth, 8)
        return strided_row(down_ref, base_down, row - depth - 8, depth)

    return first_row


INNER = {(1, 1): 0, (1, 2): 1, (1, 5): 2, (1, 6): 3, (2, 2): 4, (2, 3): 5, (2, 4): 6, (2, 5): 7, (3, 3): 8, (3, 4): 9}
INNER_PAIRS = {1: [(1, 2), (3, 4), (5, 6)], 2: [(2, 3), (4, 5)], 3: [(3, 4)]}


def outer_pairs(depth):
    pairs = {}
    for step in range(1, STEPS + 1):
        rows = [row for row in range(step, 2 * depth + 8 - step) if not step <= row - depth < 8 - step or step == STEPS]
        pairs[step] = [tuple(rows[i : i + 2]) for i in range(0, len(rows), 2)]
    return pairs


def emit_pair(member, step, pair, coef, heat, lefts, depth):
    load, store = member
    last = step == STEPS
    shift = DEEP_B - depth
    smooth = []
    rows = {}
    for row in pair:
        for at in (row - 1, row, row + 1):
            if at not in rows:
                rows[at] = load(step - 1, at)
    for row in pair:
        here = rows[row]
        at = row + shift
        total = (rows[row - 1] + rows[row + 1]) + (pltpu.roll(here, 1, 1) + pltpu.roll(here, 127, 1))
        keep = coef[0, pl.ds(at * 8, 8), :]
        diff = coef[1, pl.ds(at * 8, 8), :]
        smooth.append(jnp.concatenate([keep] * 4, 0) * here + jnp.concatenate([diff] * 4, 0) * total)
    high, low = split(jnp.concatenate(smooth, 1))
    right = jnp.concatenate([high, high, low], 0)
    mixed = jnp.dot(lefts[0 if step == 1 else 2 if last else 1], right, preferred_element_type=jnp.float32)
    for i, row in enumerate(pair):
        part = mixed[:, 128 * i : 128 * (i + 1)]
        warm = heat[1 if last else 0, pl.ds((row + shift) * 32, 32), :]
        factor = 0.05 * (part * part) if last else part * part
        store(step, row, part * (1.0 - factor) + warm)


def run_members(members, pairs, coef, heat, lefts, depth, lag=LAG):
    for wave in range(len(pairs[1]) + lag * STEPS):
        for step in pairs:
            at = wave - lag * (step - 1)
            if 0 <= at < len(pairs[step]):
                for member in members:
                    emit_pair(member, step, pairs[step][at], coef, heat, lefts, depth)


def outer_member(depth, first_row, inner_ref, state, store_last):
    def load(done, row):
        if done == 0:
            return first_row(row)
        place = INNER.get((done, row - depth)) if inner_ref is not None else None
        if place is not None:
            return inner_ref[pl.ds(place * 32, 32), :]
        return state[done % 2][pl.ds(row * 32, 32), :]

    def store(step, row, value):
        if step == STEPS:
            store_last(row - depth, value)
        else:
            state[step % 2][pl.ds(row * 32, 32), :] = value

    return load, store


def inner_member(own_ref, inner_ref, state):
    def load(done, row):
        if done == 0:
            return strided_row(own_ref, 0, row, 8)
        return state[done % 2][pl.ds(row * 32, 32), :]

    def store(step, row, value):
        if step < 3:
            state[step % 2][pl.ds(row * 32, 32), :] = value
        if (step, row) in INNER:
            inner_ref[pl.ds(INNER[step, row] * 32, 32), :] = value

    return load, store


def all_pairs(depth):
    return {step: [(row, row + 1) for row in range(step, 2 * depth + 8 - step, 2)] for step in range(1, STEPS + 1)}


def prepare(pup_ref, pdown_ref, hown_ref, diff_ref, mix_ref, coef, heat, lefts):
    for row in range(18) if pup_ref is not None else range(5, 13):
        if row < 5:
            value = strided_row(pup_ref, 0, row, 5)
            diff = pup_ref[pl.ds(150 + row, 1), :]
        elif row < 13:
            value = strided_row(hown_ref, 0, row - 5, 8)
            diff = diff_ref[pl.ds(row - 5, 1), :]
        else:
            value = strided_row(pdown_ref, 0, row - 13, 5)
            diff = pdown_ref[pl.ds(150 + row - 13, 1), :]
        heat[1, pl.ds(row * 32, 32), :] = value
        heat[0, pl.ds(row * 32, 32), :] = SCALE * value
        diff = jnp.broadcast_to(diff, (8, 128))
        coef[1, pl.ds(row * 8, 8), :] = diff
        coef[0, pl.ds(row * 8, 8), :] = 1.0 - 4.0 * diff
    mix = mix_ref[...]
    for i, factor in enumerate((SCALE, 1.0, 1.0 / SCALE)):
        high, low = split(factor * mix)
        lefts[i] = jnp.concatenate([high, low, high], 1)


def keep_scored(tq_ref, j, out):
    tq_ref[j, 0:8, :] = out[0:8, :]
    tq_ref[j, 8:16, :] = out[8 * LEV : 8 * LEV + 8, :]


def inner_kernel(f_ref, hown_ref, diff_ref, mix_ref, inner_ref, coef, heat, lefts, *states):
    @pl.when(pl.program_id(0) == 0)
    def _():
        prepare(None, None, hown_ref, diff_ref, mix_ref, coef, heat, lefts)

    def one(p, carry):
        members = [inner_member(f_ref.at[p * 4 + q], inner_ref.at[p * 4 + q], states[2 * q : 2 * q + 2]) for q in range(4)]
        run_members(members, INNER_PAIRS, coef, heat, lefts, 0, 2)
        return carry

    lax.fori_loop(0, 2, one, 0)


def chunk_a_kernel(
    f_ref, inner_ref, up_ref, down_ref, pup_ref, pdown_ref, hown_ref, diff_ref, mix_ref, out_ref, tq_ref, pup_out, pdown_out, coef, heat, lefts,
    *states,
):
    @pl.when(pl.program_id(0) == 0)
    def _():
        prepare(pup_ref, pdown_ref, hown_ref, diff_ref, mix_ref, coef, heat, lefts)
        pup_out[...] = pup_ref[...]
        pdown_out[...] = pdown_ref[...]

    def one(p, carry):
        members = []
        for q in range(2):
            j = p * 2 + q
            base = pl.multiple_of(j * 120, 8)
            rows = first_rows(DEEP_A, up_ref, base, f_ref.at[j], down_ref, base)
            last = functools.partial(strided_store, out_ref.at[j])
            members.append(outer_member(DEEP_A, rows, inner_ref.at[j], states[2 * q : 2 * q + 2], last))
        run_members(members, outer_pairs(DEEP_A), coef, heat, lefts, DEEP_A)
        for q in range(2):
            keep_scored(tq_ref, p * 2 + q, out_ref.at[p * 2 + q])
        return carry

    lax.fori_loop(0, BLK // 2, one, 0)


def chunk_b_kernel(
    f_ref, inner_ref, up_ref, down_ref, pup_ref, pdown_ref, hown_ref, diff_ref, mix_ref, prev_ref, out_ref, tq_ref, edge_ref,
    coef, heat, lefts, *states,
):
    @pl.when(pl.program_id(0) == 0)
    def _():
        prepare(pup_ref, pdown_ref, hown_ref, diff_ref, mix_ref, coef, heat, lefts)

    def store_last(j, row, value):
        if 0 <= row < 8:
            strided_store(out_ref.at[j], row, value)
            return
        slot = 0 if row < 0 else 3
        t, q = value[0:1], value[LEV : LEV + 1]
        edge_ref[j, slot : slot + 1, :] = t
        edge_ref[j, slot + 1 : slot + 2, :] = q
        edge_ref[j, slot + 2 : slot + 3, :] = t

    def one(p, carry):
        members = []
        for q in range(2):
            j = p * 2 + q
            base = j * (30 * DEEP_B)
            rows = first_rows(DEEP_B, up_ref, base, f_ref.at[j], down_ref, base)
            edge_ref[j] = jnp.zeros((8, 128), jnp.float32)
            last = functools.partial(store_last, j)
            members.append(outer_member(DEEP_B, rows, inner_ref.at[j], states[2 * q : 2 * q + 2], last))
        run_members(members, outer_pairs(DEEP_B), coef, heat, lefts, DEEP_B)
        for q in range(2):
            keep_scored(tq_ref, p * 2 + q, out_ref.at[p * 2 + q])
        return carry

    lax.fori_loop(0, BLK // 2, one, 0)


def send_rows(x_ref, up_ref, down_ref, base, depth):
    for row in range(depth):
        for start in STARTS:
            to = pl.ds(base + start * depth + row, 8, stride=depth)
            down_ref[to, :] = x_ref[pl.ds(start * 8 + row, 8, stride=8), :]
            up_ref[to, :] = x_ref[pl.ds(start * 8 + 8 - depth + row, 8, stride=8), :]


def send_members(f_ref, first, count, depth, up_ref, down_ref, buf, up_buf, down_buf, sems, before, after):
    rows = BLK * 30 * depth
    blocks = count // BLK
    fetches = [
        pltpu.make_async_copy(f_ref.at[pl.ds(first + k * BLK, BLK)], buf.at[pl.ds(k * BLK, BLK)], sems.at[k]) for k in range(blocks)
    ]
    for fetch in fetches:
        fetch.start()
    copies = []

    def put(start, size, k):
        for i, (source, target) in enumerate(((up_buf, up_ref), (down_buf, down_ref))):
            where = pl.ds(start, size)
            copies.append(pltpu.make_async_copy(source.at[where], target.at[where], sems.at[blocks + 2 * k + i]))
            copies[-1].start()

    extra = before()
    if extra:
        put(count * 30 * depth, extra, blocks)
    for k, fetch in enumerate(fetches):
        fetch.wait()

        def one(j, carry):
            m = k * BLK + j
            send_rows(buf.at[m], up_buf, down_buf, m * (30 * depth), depth)
            return carry

        lax.fori_loop(0, BLK, one, 0)
        put(k * rows, rows, k)
    after()
    for copy in copies:
        copy.wait()


def edges_a_kernel(
    me_ref, counts_ref, f_ref, heat_ref, diff_ref, land_ref, pieces_ref, up_ref, down_ref, buf, up_buf, down_buf, sems, pieces, hot_sems
):
    put_pieces = pltpu.make_async_copy(pieces, pieces_ref, hot_sems.at[1])

    def before():
        base = me_ref[0] * 32
        hot = jnp.int32(0)
        for j in range(1, 32):
            hot = jnp.where(counts_ref[base + j] >= 2, j, hot)
        pltpu.make_async_copy(f_ref.at[hot], pieces.at[pl.ds(0, 240)], hot_sems.at[0]).start()
        pieces[240:256, :] = jnp.zeros((16, 128), jnp.float32)
        base = NA * 120
        send_rows(heat_ref, up_buf, down_buf, base, 5)
        diff = diff_ref[...]
        land = land_ref[...].astype(jnp.float32)
        up_buf[base + 150 : base + 155, :] = diff[3:]
        up_buf[base + 155 : base + 160, :] = land[3:]
        down_buf[base + 150 : base + 155, :] = diff[:5]
        down_buf[base + 155 : base + 160, :] = land[:5]
        return PARAMS

    def after():
        pltpu.make_async_copy(f_ref.at[0], pieces.at[pl.ds(0, 240)], hot_sems.at[0]).wait()
        put_pieces.start()

    send_members(f_ref, 0, NA, DEEP_A, up_ref, down_ref, buf, up_buf, down_buf, sems, before, after)
    put_pieces.wait()


def edges_b_kernel(f_ref, up_ref, down_ref, buf, up_buf, down_buf, sems):
    send_members(f_ref, NA, NB, DEEP_B, up_ref, down_ref, buf, up_buf, down_buf, sems, lambda: 0, lambda: None)


def mid_kernel(donor_ref, tq_ref, up_ref, down_ref):
    for k in range(2 * NA // 8):
        up_ref[pl.ds(8 * k, 8), :] = tq_ref[pl.ds(64 * k + 7, 8, stride=8), :]
        down_ref[pl.ds(8 * k, 8), :] = tq_ref[pl.ds(64 * k, 8, stride=8), :]
    send_rows(donor_ref, up_ref, down_ref, 2 * NA, DEEP_A)


def pick_kernel(index_ref, pieces_ref, out_ref):
    for g in range(16):
        out_ref[g] = pieces_ref[index_ref[g]]


def edge_mask(pup_ref, pdown_ref):
    before, after = pup_ref[159:160, :], pdown_ref[155:156, :]
    one = jnp.ones((1, 128), jnp.float32)
    return jnp.concatenate([before, one, 1.0 - before, after, one, 1.0 - after, one, one], 0)


def score_members(count, tq_ref, edge_ref, land, mask, left, head_ref, acc, first):
    sea = 1.0 - land

    def four(p, carry):
        rights = []
        for pair in range(2):
            cols = []
            for q in range(2):
                m = p * 4 + pair * 2 + q
                t = tq_ref[m, 0:8, :]
                edge = edge_ref[pl.ds(pl.multiple_of(m * 8, 8), 8), :]
                value = jnp.concatenate([t * land, tq_ref[m, 8:16, :], t * sea, edge * mask], 0)
                cols.append(jnp.concatenate([pltpu.roll(value, 1, 1), value, pltpu.roll(value, 127, 1)], 0))
            h, l = split(jnp.concatenate(cols, 1))
            rights.append(jnp.concatenate([h, h, l], 0))
        for pair in range(2):
            total = [jnp.zeros((8, 128), jnp.float32)] * 2
            for block in range(4):
                rows = slice(64 * block, 64 * block + 64)
                hidden = jnp.maximum(jnp.dot(left[rows, :], rights[pair], preferred_element_type=jnp.float32), 0.0)
                head = head_ref[rows, :]
                for q in range(2):
                    part = (hidden[:, 128 * q : 128 * (q + 1)] * head).reshape(8, 8, 128)
                    total[q] = total[q] + jnp.sum(part, 0)
            for q in range(2):
                acc[pl.ds(first + p * 4 + pair * 2 + q, 1), :] = jnp.sum(total[q], 0, keepdims=True)
        return carry

    lax.fori_loop(0, count // 4, four, 0)


def finish_kernel(
    killed_ref, tqa_ref, before_ref, after_ref, tqb_ref, edgeb_ref, land_ref, weight_ref, head_ref, donor_ref,
    pup_ref, pdown_ref, hown_ref, diff_ref, mix_ref, prev_ref,
    out_ref, sums_ref, coef, heat, lefts, s0, s1, donor, edge, left, acc, sems,
):
    prepare(pup_ref, pdown_ref, hown_ref, diff_ref, mix_ref, coef, heat, lefts)
    rows = first_rows(DEEP_A, before_ref, 2 * NA, donor_ref, after_ref, 2 * NA)
    member = outer_member(DEEP_A, rows, None, (s0, s1), functools.partial(strided_store, donor))
    run_members([member], all_pairs(DEEP_A), coef, heat, lefts, DEEP_A)

    def copy(m):
        return pltpu.make_async_copy(donor, out_ref.at[m], sems.at[m])

    for m in range(32):
        @pl.when(killed_ref[m] > 0)
        def _():
            copy(m).start()

    zero = jnp.zeros((8, 128), jnp.float32)
    for k in range((NA + 7) // 8):
        parts = [ref[pl.ds(16 * k + i, 8, stride=2), :] for ref in (before_ref, after_ref) for i in (0, 1)]
        for slot, value in enumerate((parts[0], parts[1], parts[0], parts[2], parts[3], parts[2], zero, zero)):
            edge[pl.ds(64 * k + slot, 8, stride=8), :] = value
    high, low = split(weight_ref[...])
    left[...] = jnp.concatenate([high, low, high], 1)
    land = land_ref[...].astype(jnp.float32)
    mask = edge_mask(pup_ref, pdown_ref)
    score_members(NA, tqa_ref, edge, land, mask, left, head_ref, acc, 0)
    score_members(NB, tqb_ref, edgeb_ref, land, mask, left, head_ref, acc, NA)
    ones = jnp.ones((8, 128), jnp.float32)
    padded = jnp.concatenate([acc[...], jnp.zeros((96, 128), jnp.float32)], 0)
    sums = lax.dot_general(
        ones, padded, (((1,), (1,)), ((), ())), precision=lax.Precision.HIGHEST, preferred_element_type=jnp.float32
    )
    for k in range(16):
        sums_ref[pl.ds(8 * k, 8), :] = sums
    for m in range(32):
        @pl.when(killed_ref[m] > 0)
        def _():
            copy(m).wait()


def weight_kernel(me_ref, parts_ref, counts_ref, source_ref, scores_ref, slot_ref):
    me = me_ref[0]
    scores = jnp.sum(parts_ref[...].reshape(8, 16, 128), 0)[:, :32]
    weights = jnp.exp(scores)
    total = jnp.sum(weights)
    weights = weights / (total / 512.0)
    counts = counts_ref[...].astype(jnp.float32)
    group = lax.broadcasted_iota(jnp.int32, (16, 32), 0)
    member = lax.broadcasted_iota(jnp.int32, (16, 32), 1)
    flat = group * 32 + member
    source = source_ref[...]
    mine = group == me
    killed = jnp.logical_and(mine, source != flat)
    donor = jnp.max(jnp.where(killed, source, -1))
    here = flat == donor
    donor_weight = jnp.sum(jnp.where(here, weights, 0.0))
    donor_count = jnp.sum(jnp.where(here, counts, 0.0))
    top = jnp.where(killed, donor_weight, weights)
    under = jnp.where(killed, donor_count, counts)
    share = jnp.where(mine, top / jnp.where(mine, under, 1.0), 0.0)
    own = jnp.where(mine, scores, 0.0)
    scores_ref[...] = jnp.sum(own, 0, keepdims=True)
    slot_ref[...] = jnp.sum(share, 0, keepdims=True)


def spread_matrix():
    table = np.zeros((27, 8, 96), np.float32)
    for k in range(3):
        for a in (-1, 0, 1):
            for b in (-1, 0, 1):
                tap = 9 * k + 3 * (a + 1) + (b + 1)
                for i in range(8):
                    row = i + a
                    if 0 <= row < 8:
                        slot = 8 * k + row
                    elif row < 0:
                        slot = 24 + k
                    else:
                        slot = 27 + k
                    table[tap, i, (b + 1) * 32 + slot] = 1.0
    return table.reshape(27, 8 * 96)


GRANT = {"chunk_a": 50, "chunk_b": 53, "pick": 24, "mid": 24, "finish": 24, "weights": 24}


def call(kernel, outs, name, **kw):
    params = pltpu.CompilerParams(vmem_limit_bytes=GRANT[name] << 20) if name in GRANT else None
    return pl.pallas_call(kernel, out_shape=outs, compiler_params=params, **kw)


def f32(*shape):
    return jax.ShapeDtypeStruct(shape, jnp.float32)


def local(fields, diffusion, mixing, heating, land_mask, conv_weight, head_weight, counts, source):
    size = lax.axis_size("lat")
    up = [(i, i + 1) for i in range(size - 1)]
    down = [(i + 1, i) for i in range(size - 1)]
    me = lax.axis_index("grp").reshape(1).astype(jnp.int32)
    counts2 = counts.reshape(16, 32)
    source2 = source.reshape(16, 32)
    f = fields.reshape(32, 240, 128)
    heat = heating.reshape(240, 128)
    hbm = pl.BlockSpec(memory_space=ANY)

    def edge_scratch(count, rows):
        return [
            VMEM((count, 240, 128), jnp.float32),
            VMEM((rows, 128), jnp.float32),
            VMEM((rows, 128), jnp.float32),
            pltpu.SemaphoreType.DMA((3 * (count // BLK) + 2,)),
        ]

    rows_a = NA * 120 + PARAMS
    pieces, send_up_a, send_down_a = call(
        edges_a_kernel,
        (f32(256, 128), f32(rows_a, 128), f32(rows_a, 128)),
        in_specs=[SCALAR, SCALAR, hbm, WHOLE, WHOLE, WHOLE],
        out_specs=(hbm, hbm, hbm),
        scratch_shapes=edge_scratch(NA, rows_a) + [VMEM((256, 128), jnp.float32), pltpu.SemaphoreType.DMA((2,))],
        name="edges_a",
    )(me, counts, f, heat, diffusion, land_mask)

    pieces = lax.all_to_all(pieces.reshape(16, 16, 128), "grp", 0, 0, tiled=True)
    up_a = lax.ppermute(send_up_a, "lat", up)
    down_a = lax.ppermute(send_down_a, "lat", down)
    flat = jnp.arange(512, dtype=jnp.int32).reshape(16, 32)
    donor_group = jnp.max(jnp.where(source2 != flat, source2 // 32, 0), 1)
    pieces = call(pick_kernel, f32(16, 16, 128), in_specs=[SCALAR, WHOLE], out_specs=WHOLE, name="pick")(donor_group, pieces)
    donor_state = lax.all_to_all(pieces, "grp", 0, 0, tiled=True).reshape(256, 128)

    send_up_b, send_down_b = call(
        edges_b_kernel,
        (f32(NB * 150, 128), f32(NB * 150, 128)),
        in_specs=[hbm],
        out_specs=(hbm, hbm),
        scratch_shapes=edge_scratch(NB, NB * 150),
        name="edges_b",
    )(f)
    up_b = lax.ppermute(send_up_b, "lat", up)
    down_b = lax.ppermute(send_down_b, "lat", down)

    mix = jnp.concatenate([mixing[:24], mixing[22:]], 0)
    mix = jnp.concatenate([mix[:, :24], jnp.zeros((32, 2), jnp.float32), mix[:, 24:]], 1)
    taps = jnp.dot(conv_weight, jnp.asarray(spread_matrix()), precision=lax.Precision.HIGHEST).reshape(256, 96)
    head = head_weight.reshape(256, 128)
    killed = (lax.dynamic_index_in_dim(counts2, me[0], 0, keepdims=False) == 0).astype(jnp.int32)

    def whole(shape, at=0):
        return pl.BlockSpec(shape, lambda *i: (at,) + (0,) * (len(shape) - 1))

    params = whole((PARAMS, 128), NA * 120 // PARAMS)
    block = pl.BlockSpec((BLK, 240, 128), lambda i: (i, 0, 0))
    tq_block = pl.BlockSpec((BLK, 16, 128), lambda i: (i, 0, 0))
    step_scratch = [
        VMEM((2, 18 * 8, 128), jnp.float32),
        VMEM((2, 18 * 32, 128), jnp.float32),
        VMEM((3, 32, 96), jnp.bfloat16),
    ] + [VMEM((18 * 32, 128), jnp.float32)] * 4
    shared = [params, params, WHOLE, WHOLE, WHOLE]
    halo_a = pl.BlockSpec((BLK * 30 * DEEP_A, 128), lambda i: (i, 0))
    whole_params = whole((PARAMS, 128))
    inner = call(
        inner_kernel,
        f32(32, 320, 128),
        grid=(4,),
        in_specs=[pl.BlockSpec((8, 240, 128), lambda i: (i, 0, 0))] + [WHOLE] * 3,
        out_specs=pl.BlockSpec((8, 320, 128), lambda i: (i, 0, 0)),
        scratch_shapes=step_scratch[:3] + [VMEM((8 * 32, 128), jnp.float32)] * 8,
        cost_estimate=pl.CostEstimate(flops=1 << 32, bytes_accessed=10 << 20, transcendentals=0),
        name="inner",
    )(f, heat, diffusion, mix)
    inner_block = pl.BlockSpec((BLK, 320, 128), lambda i: (i, 0, 0))
    inner_b = pl.BlockSpec((BLK, 320, 128), lambda i: (i + NA // BLK, 0, 0))
    state_a, tq_a, params_up, params_down = call(
        chunk_a_kernel,
        (f32(32, 240, 128), f32(NA, 16, 128), f32(PARAMS, 128), f32(PARAMS, 128)),
        grid=(NA // BLK,),
        in_specs=[block, inner_block, halo_a, halo_a] + shared,
        out_specs=(block, tq_block, whole_params, whole_params),
        scratch_shapes=step_scratch,
        name="chunk_a",
    )(f, inner, up_a, down_a, up_a, down_a, heat, diffusion, mix)

    send_up, send_down = call(
        mid_kernel, (f32(MID, 128), f32(MID, 128)), in_specs=[WHOLE, WHOLE], out_specs=(WHOLE, WHOLE), name="mid"
    )(donor_state, tq_a.reshape(NA * 16, 128))
    before = lax.ppermute(send_up, "lat", up)
    after = lax.ppermute(send_down, "lat", down)

    halo_b = pl.BlockSpec((BLK * 30 * DEEP_B, 128), lambda i: (i, 0))
    block_b = pl.BlockSpec((BLK, 240, 128), lambda i: (i + NA // BLK, 0, 0))
    state_b, tq_b, edge_b = call(
        chunk_b_kernel,
        (f32(32, 240, 128), f32(NB, 16, 128), f32(NB, 8, 128)),
        grid=(NB // BLK,),
        in_specs=[block_b, inner_b, halo_b, halo_b] + [WHOLE] * 5 + [hbm],
        out_specs=(block_b, tq_block, pl.BlockSpec((BLK, 8, 128), lambda i: (i, 0, 0))),
        scratch_shapes=step_scratch,
        input_output_aliases={9: 0},
        name="chunk_b",
    )(f, inner, up_b, down_b, params_up, params_down, heat, diffusion, mix, state_a)

    new_fields, sums = call(
        finish_kernel,
        (f32(32, 240, 128), f32(128, 128)),
        grid=(1,),
        in_specs=[SCALAR] + [WHOLE] * 14 + [hbm],
        out_specs=(hbm, WHOLE),
        scratch_shapes=step_scratch[:-2]
        + [
            VMEM((240, 128), jnp.float32),
            VMEM(((NA + 7) // 8 * 64, 128), jnp.float32),
            VMEM((256, 288), jnp.bfloat16),
            VMEM((32, 128), jnp.float32),
            pltpu.SemaphoreType.DMA((32,)),
        ],
        input_output_aliases={15: 0},
        name="finish",
    )(
        killed, tq_a, before, after, tq_b, edge_b.reshape(NB * 8, 128), land_mask, taps, head, donor_state,
        params_up, params_down, heat, diffusion, mix, state_b,
    )

    parts = lax.all_to_all(sums.reshape(128, 1, 128), ("lat", "grp"), 0, 0, tiled=True)
    scores, slot = call(
        weight_kernel, (f32(1, 32), f32(1, 32)), in_specs=[SCALAR] + [WHOLE] * 3, out_specs=(WHOLE, WHOLE), name="weights"
    )(me, parts.reshape(128, 128), counts2, source2)
    return new_fields.reshape(32, 30, 8, 128), scores.reshape(32), slot.reshape(32)


def solution(mesh):
    return jax.shard_map(
        local,
        mesh=mesh,
        in_specs=(
            P("grp", None, "lat", None),
            P("lat", None),
            P(),
            P(None, "lat", None),
            P("lat", None),
            P(),
            P(None, "lat", None),
            P(),
            P(),
        ),
        out_specs=(P("grp", None, "lat", None), P("grp"), P("grp")),
        check_vma=False,
    )
```

```python
import functools

import jax
import jax.numpy as jnp
import numpy as np
from jax import lax
from jax.experimental import pallas as pl
from jax.experimental.pallas import tpu as pltpu
from jax.sharding import PartitionSpec as P


LEV = 10
STEPS = 4
STARTS = (0, 8, 16, 22)
DEEP_A = 4
DEEP_B = 5
NA = 20
NB = 32 - NA
BLK = 4
PARAMS = 160
MID = 2 * NA + 120
SCALE = 0.05**0.5
LAG = 4


VMEM = pltpu.VMEM
ANY = pl.ANY
WHOLE = pl.BlockSpec(memory_space=pltpu.VMEM)
SCALAR = pl.BlockSpec(memory_space=pltpu.SMEM)


def split(value):
    high = value.astype(jnp.bfloat16)
    low = (value - high.astype(jnp.float32)).astype(jnp.bfloat16)
    return high, low


def strided_row(ref, base, row, stride):
    parts = [ref[pl.ds(base + start * stride + row, 8, stride=stride), :] for start in STARTS]
    return jnp.concatenate(parts, 0)


def strided_store(ref, row, value):
    for k, start in enumerate(STARTS):
        ref[pl.ds(start * 8 + row, 8, stride=8), :] = value[8 * k : 8 * k + 8]


def first_rows(depth, up_ref, base_up, own_ref, down_ref, base_down):
    def first_row(row):
        if row < depth:
            return strided_row(up_ref, base_up, row, depth)
        if row < depth + 8:
            return strided_row(own_ref, 0, row - depth, 8)
        return strided_row(down_ref, base_down, row - depth - 8, depth)

    return first_row


INNER = {(1, 1): 0, (1, 2): 1, (1, 5): 2, (1, 6): 3, (2, 2): 4, (2, 3): 5, (2, 4): 6, (2, 5): 7, (3, 3): 8, (3, 4): 9}
INNER_PAIRS = {1: [(1, 2), (3, 4), (5, 6)], 2: [(2, 3), (4, 5)], 3: [(3, 4)]}


def outer_pairs(depth):
    pairs = {}
    for step in range(1, STEPS + 1):
        rows = [row for row in range(step, 2 * depth + 8 - step) if not step <= row - depth < 8 - step or step == STEPS]
        pairs[step] = [tuple(rows[i : i + 2]) for i in range(0, len(rows), 2)]
    return pairs


def emit_pair(member, step, pair, coef, heat, lefts, depth):
    load, store = member
    last = step == STEPS
    shift = DEEP_B - depth
    smooth = []
    rows = {}
    for row in pair:
        for at in (row - 1, row, row + 1):
            if at not in rows:
                rows[at] = load(step - 1, at)
    for row in pair:
        here = rows[row]
        at = row + shift
        total = (rows[row - 1] + rows[row + 1]) + (pltpu.roll(here, 1, 1) + pltpu.roll(here, 127, 1))
        keep = coef[0, pl.ds(at * 8, 8), :]
        diff = coef[1, pl.ds(at * 8, 8), :]
        smooth.append(jnp.concatenate([keep] * 4, 0) * here + jnp.concatenate([diff] * 4, 0) * total)
    high, low = split(jnp.concatenate(smooth, 1))
    right = jnp.concatenate([high, high, low], 0)
    mixed = jnp.dot(lefts[0 if step == 1 else 2 if last else 1], right, preferred_element_type=jnp.float32)
    for i, row in enumerate(pair):
        part = mixed[:, 128 * i : 128 * (i + 1)]
        warm = heat[1 if last else 0, pl.ds((row + shift) * 32, 32), :]
        factor = 0.05 * (part * part) if last else part * part
        store(step, row, part * (1.0 - factor) + warm)


def run_members(members, pairs, coef, heat, lefts, depth, lag=LAG):
    for wave in range(len(pairs[1]) + lag * STEPS):
        for step in pairs:
            at = wave - lag * (step - 1)
            if 0 <= at < len(pairs[step]):
                for member in members:
                    emit_pair(member, step, pairs[step][at], coef, heat, lefts, depth)


def outer_member(depth, first_row, inner_ref, state, store_last):
    def load(done, row):
        if done == 0:
            return first_row(row)
        place = INNER.get((done, row - depth)) if inner_ref is not None else None
        if place is not None:
            return inner_ref[pl.ds(place * 32, 32), :]
        return state[done % 2][pl.ds(row * 32, 32), :]

    def store(step, row, value):
        if step == STEPS:
            store_last(row - depth, value)
        else:
            state[step % 2][pl.ds(row * 32, 32), :] = value

    return load, store


def inner_member(own_ref, inner_ref, state):
    def load(done, row):
        if done == 0:
            return strided_row(own_ref, 0, row, 8)
        return state[done % 2][pl.ds(row * 32, 32), :]

    def store(step, row, value):
        if step < 3:
            state[step % 2][pl.ds(row * 32, 32), :] = value
        if (step, row) in INNER:
            inner_ref[pl.ds(INNER[step, row] * 32, 32), :] = value

    return load, store


def all_pairs(depth):
    return {step: [(row, row + 1) for row in range(step, 2 * depth + 8 - step, 2)] for step in range(1, STEPS + 1)}


def prepare(pup_ref, pdown_ref, hown_ref, diff_ref, mix_ref, coef, heat, lefts):
    for row in range(18) if pup_ref is not None else range(5, 13):
        if row < 5:
            value = strided_row(pup_ref, 0, row, 5)
            diff = pup_ref[pl.ds(150 + row, 1), :]
        elif row < 13:
            value = strided_row(hown_ref, 0, row - 5, 8)
            diff = diff_ref[pl.ds(row - 5, 1), :]
        else:
            value = strided_row(pdown_ref, 0, row - 13, 5)
            diff = pdown_ref[pl.ds(150 + row - 13, 1), :]
        heat[1, pl.ds(row * 32, 32), :] = value
        heat[0, pl.ds(row * 32, 32), :] = SCALE * value
        diff = jnp.broadcast_to(diff, (8, 128))
        coef[1, pl.ds(row * 8, 8), :] = diff
        coef[0, pl.ds(row * 8, 8), :] = 1.0 - 4.0 * diff
    mix = mix_ref[...]
    for i, factor in enumerate((SCALE, 1.0, 1.0 / SCALE)):
        high, low = split(factor * mix)
        lefts[i] = jnp.concatenate([high, low, high], 1)


def keep_scored(tq_ref, j, out):
    tq_ref[j, 0:8, :] = out[0:8, :]
    tq_ref[j, 8:16, :] = out[8 * LEV : 8 * LEV + 8, :]


def inner_kernel(f_ref, hown_ref, diff_ref, mix_ref, inner_ref, coef, heat, lefts, *states):
    @pl.when(pl.program_id(0) == 0)
    def _():
        prepare(None, None, hown_ref, diff_ref, mix_ref, coef, heat, lefts)

    def one(p, carry):
        members = [inner_member(f_ref.at[p * 4 + q], inner_ref.at[p * 4 + q], states[2 * q : 2 * q + 2]) for q in range(4)]
        run_members(members, INNER_PAIRS, coef, heat, lefts, 0, 2)
        return carry

    lax.fori_loop(0, 2, one, 0)


def chunk_a_kernel(
    f_ref, inner_ref, up_ref, down_ref, pup_ref, pdown_ref, hown_ref, diff_ref, mix_ref, out_ref, tq_ref, pup_out, pdown_out, coef, heat, lefts,
    *states,
):
    @pl.when(pl.program_id(0) == 0)
    def _():
        prepare(pup_ref, pdown_ref, hown_ref, diff_ref, mix_ref, coef, heat, lefts)
        pup_out[...] = pup_ref[...]
        pdown_out[...] = pdown_ref[...]

    def one(p, carry):
        members = []
        for q in range(4):
            j = p * 4 + q
            base = pl.multiple_of(j * 120, 8)
            rows = first_rows(DEEP_A, up_ref, base, f_ref.at[j], down_ref, base)
            last = functools.partial(strided_store, out_ref.at[j])
            members.append(outer_member(DEEP_A, rows, inner_ref.at[j], states[2 * q : 2 * q + 2], last))
        run_members(members, outer_pairs(DEEP_A), coef, heat, lefts, DEEP_A)
        for q in range(4):
            keep_scored(tq_ref, p * 4 + q, out_ref.at[p * 4 + q])
        return carry

    lax.fori_loop(0, BLK // 4, one, 0)


def chunk_b_kernel(
    f_ref, inner_ref, up_ref, down_ref, pup_ref, pdown_ref, hown_ref, diff_ref, mix_ref, prev_ref, out_ref, tq_ref, edge_ref,
    coef, heat, lefts, *states,
):
    @pl.when(pl.program_id(0) == 0)
    def _():
        prepare(pup_ref, pdown_ref, hown_ref, diff_ref, mix_ref, coef, heat, lefts)

    def store_last(j, row, value):
        if 0 <= row < 8:
            strided_store(out_ref.at[j], row, value)
            return
        slot = 0 if row < 0 else 3
        t, q = value[0:1], value[LEV : LEV + 1]
        edge_ref[j, slot : slot + 1, :] = t
        edge_ref[j, slot + 1 : slot + 2, :] = q
        edge_ref[j, slot + 2 : slot + 3, :] = t

    def one(p, carry):
        members = []
        for q in range(4):
            j = p * 4 + q
            base = j * (30 * DEEP_B)
            rows = first_rows(DEEP_B, up_ref, base, f_ref.at[j], down_ref, base)
            edge_ref[j] = jnp.zeros((8, 128), jnp.float32)
            last = functools.partial(store_last, j)
            members.append(outer_member(DEEP_B, rows, inner_ref.at[j], states[2 * q : 2 * q + 2], last))
        run_members(members, outer_pairs(DEEP_B), coef, heat, lefts, DEEP_B)
        for q in range(4):
            keep_scored(tq_ref, p * 4 + q, out_ref.at[p * 4 + q])
        return carry

    lax.fori_loop(0, BLK // 4, one, 0)


def send_rows(x_ref, up_ref, down_ref, base, depth):
    for row in range(depth):
        for start in STARTS:
            to = pl.ds(base + start * depth + row, 8, stride=depth)
            down_ref[to, :] = x_ref[pl.ds(start * 8 + row, 8, stride=8), :]
            up_ref[to, :] = x_ref[pl.ds(start * 8 + 8 - depth + row, 8, stride=8), :]


def send_members(f_ref, first, count, depth, up_ref, down_ref, buf, up_buf, down_buf, sems, before, after):
    rows = BLK * 30 * depth
    blocks = count // BLK
    fetches = [
        pltpu.make_async_copy(f_ref.at[pl.ds(first + k * BLK, BLK)], buf.at[pl.ds(k * BLK, BLK)], sems.at[k]) for k in range(blocks)
    ]
    for fetch in fetches:
        fetch.start()
    copies = []

    def put(start, size, k):
        for i, (source, target) in enumerate(((up_buf, up_ref), (down_buf, down_ref))):
            where = pl.ds(start, size)
            copies.append(pltpu.make_async_copy(source.at[where], target.at[where], sems.at[blocks + 2 * k + i]))
            copies[-1].start()

    extra = before()
    if extra:
        put(count * 30 * depth, extra, blocks)
    for k, fetch in enumerate(fetches):
        fetch.wait()

        def one(j, carry):
            m = k * BLK + j
            send_rows(buf.at[m], up_buf, down_buf, m * (30 * depth), depth)
            return carry

        lax.fori_loop(0, BLK, one, 0)
        put(k * rows, rows, k)
    after()
    for copy in copies:
        copy.wait()


def edges_a_kernel(
    me_ref, counts_ref, f_ref, heat_ref, diff_ref, land_ref, pieces_ref, up_ref, down_ref, buf, up_buf, down_buf, sems, pieces, hot_sems
):
    put_pieces = pltpu.make_async_copy(pieces, pieces_ref, hot_sems.at[1])

    def before():
        base = me_ref[0] * 32
        hot = jnp.int32(0)
        for j in range(1, 32):
            hot = jnp.where(counts_ref[base + j] >= 2, j, hot)
        pltpu.make_async_copy(f_ref.at[hot], pieces.at[pl.ds(0, 240)], hot_sems.at[0]).start()
        pieces[240:256, :] = jnp.zeros((16, 128), jnp.float32)
        base = NA * 120
        send_rows(heat_ref, up_buf, down_buf, base, 5)
        diff = diff_ref[...]
        land = land_ref[...].astype(jnp.float32)
        up_buf[base + 150 : base + 155, :] = diff[3:]
        up_buf[base + 155 : base + 160, :] = land[3:]
        down_buf[base + 150 : base + 155, :] = diff[:5]
        down_buf[base + 155 : base + 160, :] = land[:5]
        return PARAMS

    def after():
        pltpu.make_async_copy(f_ref.at[0], pieces.at[pl.ds(0, 240)], hot_sems.at[0]).wait()
        put_pieces.start()

    send_members(f_ref, 0, NA, DEEP_A, up_ref, down_ref, buf, up_buf, down_buf, sems, before, after)
    put_pieces.wait()


def edges_b_kernel(f_ref, up_ref, down_ref, buf, up_buf, down_buf, sems):
    send_members(f_ref, NA, NB, DEEP_B, up_ref, down_ref, buf, up_buf, down_buf, sems, lambda: 0, lambda: None)


def mid_kernel(donor_ref, tq_ref, up_ref, down_ref):
    for k in range(2 * NA // 8):
        up_ref[pl.ds(8 * k, 8), :] = tq_ref[pl.ds(64 * k + 7, 8, stride=8), :]
        down_ref[pl.ds(8 * k, 8), :] = tq_ref[pl.ds(64 * k, 8, stride=8), :]
    send_rows(donor_ref, up_ref, down_ref, 2 * NA, DEEP_A)


def pick_kernel(index_ref, pieces_ref, out_ref):
    for g in range(16):
        out_ref[g] = pieces_ref[index_ref[g]]


def edge_mask(pup_ref, pdown_ref):
    before, after = pup_ref[159:160, :], pdown_ref[155:156, :]
    one = jnp.ones((1, 128), jnp.float32)
    return jnp.concatenate([before, one, 1.0 - before, after, one, 1.0 - after, one, one], 0)


def score_members(count, tq_ref, edge_ref, land, mask, left, head_ref, acc, first):
    sea = 1.0 - land

    def four(p, carry):
        rights = []
        for pair in range(2):
            cols = []
            for q in range(2):
                m = p * 4 + pair * 2 + q
                t = tq_ref[m, 0:8, :]
                edge = edge_ref[pl.ds(pl.multiple_of(m * 8, 8), 8), :]
                value = jnp.concatenate([t * land, tq_ref[m, 8:16, :], t * sea, edge * mask], 0)
                cols.append(jnp.concatenate([pltpu.roll(value, 1, 1), value, pltpu.roll(value, 127, 1)], 0))
            h, l = split(jnp.concatenate(cols, 1))
            rights.append(jnp.concatenate([h, h, l], 0))
        for pair in range(2):
            total = [jnp.zeros((8, 128), jnp.float32)] * 2
            for block in range(4):
                rows = slice(64 * block, 64 * block + 64)
                hidden = jnp.maximum(jnp.dot(left[rows, :], rights[pair], preferred_element_type=jnp.float32), 0.0)
                head = head_ref[rows, :]
                for q in range(2):
                    part = (hidden[:, 128 * q : 128 * (q + 1)] * head).reshape(8, 8, 128)
                    total[q] = total[q] + jnp.sum(part, 0)
            for q in range(2):
                acc[pl.ds(first + p * 4 + pair * 2 + q, 1), :] = jnp.sum(total[q], 0, keepdims=True)
        return carry

    lax.fori_loop(0, count // 4, four, 0)


def finish_kernel(
    killed_ref, tqa_ref, before_ref, after_ref, tqb_ref, edgeb_ref, land_ref, weight_ref, head_ref, donor_ref,
    pup_ref, pdown_ref, hown_ref, diff_ref, mix_ref, prev_ref,
    out_ref, sums_ref, coef, heat, lefts, s0, s1, donor, edge, left, acc, sems,
):
    prepare(pup_ref, pdown_ref, hown_ref, diff_ref, mix_ref, coef, heat, lefts)
    rows = first_rows(DEEP_A, before_ref, 2 * NA, donor_ref, after_ref, 2 * NA)
    member = outer_member(DEEP_A, rows, None, (s0, s1), functools.partial(strided_store, donor))
    run_members([member], all_pairs(DEEP_A), coef, heat, lefts, DEEP_A)

    def copy(m):
        return pltpu.make_async_copy(donor, out_ref.at[m], sems.at[m])

    for m in range(32):
        @pl.when(killed_ref[m] > 0)
        def _():
            copy(m).start()

    zero = jnp.zeros((8, 128), jnp.float32)
    for k in range((NA + 7) // 8):
        parts = [ref[pl.ds(16 * k + i, 8, stride=2), :] for ref in (before_ref, after_ref) for i in (0, 1)]
        for slot, value in enumerate((parts[0], parts[1], parts[0], parts[2], parts[3], parts[2], zero, zero)):
            edge[pl.ds(64 * k + slot, 8, stride=8), :] = value
    high, low = split(weight_ref[...])
    left[...] = jnp.concatenate([high, low, high], 1)
    land = land_ref[...].astype(jnp.float32)
    mask = edge_mask(pup_ref, pdown_ref)
    score_members(NA, tqa_ref, edge, land, mask, left, head_ref, acc, 0)
    score_members(NB, tqb_ref, edgeb_ref, land, mask, left, head_ref, acc, NA)
    ones = jnp.ones((8, 128), jnp.float32)
    padded = jnp.concatenate([acc[...], jnp.zeros((96, 128), jnp.float32)], 0)
    sums = lax.dot_general(
        ones, padded, (((1,), (1,)), ((), ())), precision=lax.Precision.HIGHEST, preferred_element_type=jnp.float32
    )
    for k in range(16):
        sums_ref[pl.ds(8 * k, 8), :] = sums
    for m in range(32):
        @pl.when(killed_ref[m] > 0)
        def _():
            copy(m).wait()


def weight_kernel(me_ref, parts_ref, counts_ref, source_ref, scores_ref, slot_ref):
    me = me_ref[0]
    scores = jnp.sum(parts_ref[...].reshape(8, 16, 128), 0)[:, :32]
    weights = jnp.exp(scores)
    total = jnp.sum(weights)
    weights = weights / (total / 512.0)
    counts = counts_ref[...].astype(jnp.float32)
    group = lax.broadcasted_iota(jnp.int32, (16, 32), 0)
    member = lax.broadcasted_iota(jnp.int32, (16, 32), 1)
    flat = group * 32 + member
    source = source_ref[...]
    mine = group == me
    killed = jnp.logical_and(mine, source != flat)
    donor = jnp.max(jnp.where(killed, source, -1))
    here = flat == donor
    donor_weight = jnp.sum(jnp.where(here, weights, 0.0))
    donor_count = jnp.sum(jnp.where(here, counts, 0.0))
    top = jnp.where(killed, donor_weight, weights)
    under = jnp.where(killed, donor_count, counts)
    share = jnp.where(mine, top / jnp.where(mine, under, 1.0), 0.0)
    own = jnp.where(mine, scores, 0.0)
    scores_ref[...] = jnp.sum(own, 0, keepdims=True)
    slot_ref[...] = jnp.sum(share, 0, keepdims=True)


def spread_matrix():
    table = np.zeros((27, 8, 96), np.float32)
    for k in range(3):
        for a in (-1, 0, 1):
            for b in (-1, 0, 1):
                tap = 9 * k + 3 * (a + 1) + (b + 1)
                for i in range(8):
                    row = i + a
                    if 0 <= row < 8:
                        slot = 8 * k + row
                    elif row < 0:
                        slot = 24 + k
                    else:
                        slot = 27 + k
                    table[tap, i, (b + 1) * 32 + slot] = 1.0
    return table.reshape(27, 8 * 96)


GRANT = {"chunk_a": 50, "chunk_b": 53, "pick": 24, "mid": 24, "finish": 24, "weights": 24}


def call(kernel, outs, name, **kw):
    params = pltpu.CompilerParams(vmem_limit_bytes=GRANT[name] << 20) if name in GRANT else None
    return pl.pallas_call(kernel, out_shape=outs, compiler_params=params, **kw)


def f32(*shape):
    return jax.ShapeDtypeStruct(shape, jnp.float32)


def local(fields, diffusion, mixing, heating, land_mask, conv_weight, head_weight, counts, source):
    size = lax.axis_size("lat")
    up = [(i, i + 1) for i in range(size - 1)]
    down = [(i + 1, i) for i in range(size - 1)]
    me = lax.axis_index("grp").reshape(1).astype(jnp.int32)
    counts2 = counts.reshape(16, 32)
    source2 = source.reshape(16, 32)
    f = fields.reshape(32, 240, 128)
    heat = heating.reshape(240, 128)
    hbm = pl.BlockSpec(memory_space=ANY)

    def edge_scratch(count, rows):
        return [
            VMEM((count, 240, 128), jnp.float32),
            VMEM((rows, 128), jnp.float32),
            VMEM((rows, 128), jnp.float32),
            pltpu.SemaphoreType.DMA((3 * (count // BLK) + 2,)),
        ]

    rows_a = NA * 120 + PARAMS
    pieces, send_up_a, send_down_a = call(
        edges_a_kernel,
        (f32(256, 128), f32(rows_a, 128), f32(rows_a, 128)),
        in_specs=[SCALAR, SCALAR, hbm, WHOLE, WHOLE, WHOLE],
        out_specs=(hbm, hbm, hbm),
        scratch_shapes=edge_scratch(NA, rows_a) + [VMEM((256, 128), jnp.float32), pltpu.SemaphoreType.DMA((2,))],
        name="edges_a",
    )(me, counts, f, heat, diffusion, land_mask)

    pieces = lax.all_to_all(pieces.reshape(16, 16, 128), "grp", 0, 0, tiled=True)
    up_a = lax.ppermute(send_up_a, "lat", up)
    down_a = lax.ppermute(send_down_a, "lat", down)
    flat = jnp.arange(512, dtype=jnp.int32).reshape(16, 32)
    donor_group = jnp.max(jnp.where(source2 != flat, source2 // 32, 0), 1)
    pieces = call(pick_kernel, f32(16, 16, 128), in_specs=[SCALAR, WHOLE], out_specs=WHOLE, name="pick")(donor_group, pieces)
    donor_state = lax.all_to_all(pieces, "grp", 0, 0, tiled=True).reshape(256, 128)

    send_up_b, send_down_b = call(
        edges_b_kernel,
        (f32(NB * 150, 128), f32(NB * 150, 128)),
        in_specs=[hbm],
        out_specs=(hbm, hbm),
        scratch_shapes=edge_scratch(NB, NB * 150),
        name="edges_b",
    )(f)
    up_b = lax.ppermute(send_up_b, "lat", up)
    down_b = lax.ppermute(send_down_b, "lat", down)

    mix = jnp.concatenate([mixing[:24], mixing[22:]], 0)
    mix = jnp.concatenate([mix[:, :24], jnp.zeros((32, 2), jnp.float32), mix[:, 24:]], 1)
    taps = jnp.dot(conv_weight, jnp.asarray(spread_matrix()), precision=lax.Precision.HIGHEST).reshape(256, 96)
    head = head_weight.reshape(256, 128)
    killed = (lax.dynamic_index_in_dim(counts2, me[0], 0, keepdims=False) == 0).astype(jnp.int32)

    def whole(shape, at=0):
        return pl.BlockSpec(shape, lambda *i: (at,) + (0,) * (len(shape) - 1))

    params = whole((PARAMS, 128), NA * 120 // PARAMS)
    block = pl.BlockSpec((BLK, 240, 128), lambda i: (i, 0, 0))
    tq_block = pl.BlockSpec((BLK, 16, 128), lambda i: (i, 0, 0))
    step_scratch = [
        VMEM((2, 18 * 8, 128), jnp.float32),
        VMEM((2, 18 * 32, 128), jnp.float32),
        VMEM((3, 32, 96), jnp.bfloat16),
    ] + [VMEM((18 * 32, 128), jnp.float32)] * 8
    shared = [params, params, WHOLE, WHOLE, WHOLE]
    halo_a = pl.BlockSpec((BLK * 30 * DEEP_A, 128), lambda i: (i, 0))
    whole_params = whole((PARAMS, 128))
    inner = call(
        inner_kernel,
        f32(32, 320, 128),
        grid=(4,),
        in_specs=[pl.BlockSpec((8, 240, 128), lambda i: (i, 0, 0))] + [WHOLE] * 3,
        out_specs=pl.BlockSpec((8, 320, 128), lambda i: (i, 0, 0)),
        scratch_shapes=step_scratch[:3] + [VMEM((8 * 32, 128), jnp.float32)] * 8,
        cost_estimate=pl.CostEstimate(flops=1 << 32, bytes_accessed=10 << 20, transcendentals=0),
        name="inner",
    )(f, heat, diffusion, mix)
    inner_block = pl.BlockSpec((BLK, 320, 128), lambda i: (i, 0, 0))
    inner_b = pl.BlockSpec((BLK, 320, 128), lambda i: (i + NA // BLK, 0, 0))
    state_a, tq_a, params_up, params_down = call(
        chunk_a_kernel,
        (f32(32, 240, 128), f32(NA, 16, 128), f32(PARAMS, 128), f32(PARAMS, 128)),
        grid=(NA // BLK,),
        in_specs=[block, inner_block, halo_a, halo_a] + shared,
        out_specs=(block, tq_block, whole_params, whole_params),
        scratch_shapes=step_scratch,
        name="chunk_a",
    )(f, inner, up_a, down_a, up_a, down_a, heat, diffusion, mix)

    send_up, send_down = call(
        mid_kernel, (f32(MID, 128), f32(MID, 128)), in_specs=[WHOLE, WHOLE], out_specs=(WHOLE, WHOLE), name="mid"
    )(donor_state, tq_a.reshape(NA * 16, 128))
    before = lax.ppermute(send_up, "lat", up)
    after = lax.ppermute(send_down, "lat", down)

    halo_b = pl.BlockSpec((BLK * 30 * DEEP_B, 128), lambda i: (i, 0))
    block_b = pl.BlockSpec((BLK, 240, 128), lambda i: (i + NA // BLK, 0, 0))
    state_b, tq_b, edge_b = call(
        chunk_b_kernel,
        (f32(32, 240, 128), f32(NB, 16, 128), f32(NB, 8, 128)),
        grid=(NB // BLK,),
        in_specs=[block_b, inner_b, halo_b, halo_b] + [WHOLE] * 5 + [hbm],
        out_specs=(block_b, tq_block, pl.BlockSpec((BLK, 8, 128), lambda i: (i, 0, 0))),
        scratch_shapes=step_scratch,
        input_output_aliases={9: 0},
        name="chunk_b",
    )(f, inner, up_b, down_b, params_up, params_down, heat, diffusion, mix, state_a)

    new_fields, sums = call(
        finish_kernel,
        (f32(32, 240, 128), f32(128, 128)),
        grid=(1,),
        in_specs=[SCALAR] + [WHOLE] * 14 + [hbm],
        out_specs=(hbm, WHOLE),
        scratch_shapes=step_scratch[:5]
        + [
            VMEM((240, 128), jnp.float32),
            VMEM(((NA + 7) // 8 * 64, 128), jnp.float32),
            VMEM((256, 288), jnp.bfloat16),
            VMEM((32, 128), jnp.float32),
            pltpu.SemaphoreType.DMA((32,)),
        ],
        input_output_aliases={15: 0},
        name="finish",
    )(
        killed, tq_a, before, after, tq_b, edge_b.reshape(NB * 8, 128), land_mask, taps, head, donor_state,
        params_up, params_down, heat, diffusion, mix, state_b,
    )

    parts = lax.all_to_all(sums.reshape(128, 1, 128), ("lat", "grp"), 0, 0, tiled=True)
    scores, slot = call(
        weight_kernel, (f32(1, 32), f32(1, 32)), in_specs=[SCALAR] + [WHOLE] * 3, out_specs=(WHOLE, WHOLE), name="weights"
    )(me, parts.reshape(128, 128), counts2, source2)
    return new_fields.reshape(32, 30, 8, 128), scores.reshape(32), slot.reshape(32)


def solution(mesh):
    return jax.shard_map(
        local,
        mesh=mesh,
        in_specs=(
            P("grp", None, "lat", None),
            P("lat", None),
            P(),
            P(None, "lat", None),
            P("lat", None),
            P(),
            P(None, "lat", None),
            P(),
            P(),
        ),
        out_specs=(P("grp", None, "lat", None), P("grp"), P("grp")),
        check_vma=False,
    )
```
